32 devices in a mesh: fem: 2 (over y), row: 4 (over x, core), col: 4 (over z).
Axes of the slice: x: 2, y: 2, z: 4, core: 2. Of those that a mesh axis runs over, the one named last changes fastest.
Arguments:
- inverse_factor: bfloat16 [32, 1536, 1536], P(('fem', 'row', 'col')), may hold values from -1 to 1.5, as said below
- coupling: bfloat16 [32, 1536, 1024], P(('fem', 'row', 'col')), may hold values from -0.19921875 to 0.19921875
- boundary_tiles: int32 [32, 8], replicated, may hold values from 0 to 15, as said below
- bem_block: float32 [8, 8, 128, 8192], P(None, ('fem', 'row'), None, 'col'), may hold values from -6 to 48
Outputs:
- boundary_factors: float32 [8, 8, 128, 8192], P(None, ('fem', 'row'), None, 'col')
The draws below stay inside these ranges and needn't reach their ends.
Inputs may be any that keep to these rules, and one draw needn't show every extreme that they name: `inverse_factor`: lower triangular. `boundary_tiles`: each row holds 8 distinct values.
All inputs are finite; a program needn't handle non-finite values.
Results may differ from the reference program's by a relative error of at most 0.0003.
Values may be sent and summed in bfloat16 or wider, within the bound.
No kernel may reach another device: no remote copies, remote signals or barrier semaphores. Data moves between devices by JAX's collectives and lax.ppermute only.
A program may use at most 128 MiB of HBM per device.

```python
import math
import jax
import jax.numpy as jnp
from jax import lax

NB = 8192
TILE = 128
FEMDOF = 1536
BROWS = 1024
PW = 256
PANELS = 1
SUBS = 32
NFR = 8
KC = 8
QN = 16
SLOTS = 8
N_ROW = 4
N_COL = 4


def draw_inverse_factor(key, part):
    subkeys = jax.random.split(jax.random.fold_in(key, 11), SUBS)

    def single(subkey):
        first_key, second_key = jax.random.split(subkey)
        values = jnp.clip(jax.random.normal(first_key, (FEMDOF, FEMDOF), jnp.float32), -6.0, 6.0)
        values = values / math.sqrt(FEMDOF)
        diagonal = jax.random.uniform(second_key, (FEMDOF,), jnp.float32, 0.5, 1.5)
        return (jnp.tril(values, -1) + jnp.diag(diagonal)).astype(jnp.bfloat16)
    return lax.map(single, subkeys)


def draw_boundary_tiles(key, part):
    subkeys = jax.random.split(jax.random.fold_in(key, 23), SUBS)

    def single(subkey):
        return jax.random.permutation(subkey, QN)[:SLOTS].astype(jnp.int32)
    return jax.vmap(single)(subkeys)


def draw_bem_block(key, part):
    first_key, second_key = jax.random.split(jax.random.fold_in(key, 37))
    values = jnp.clip(jax.random.normal(first_key, (NB, NB), jnp.float32), -6.0, 6.0)
    diagonal = jax.random.uniform(second_key, (NB,), jnp.float32, 32.0, 48.0)
    indices = jnp.arange(NB)
    values = values.at[indices, indices].set(diagonal)
    return values.reshape(KC, NFR, TILE, NB)


def steps_of(own_key, shape, shards, least, high):
    def one(dim, shards_of):
        draws = jax.random.uniform(jax.random.fold_in(jax.random.fold_in(own_key, 6), dim), (shards_of,), jnp.float32, least / len(shards), high / len(shards))
        return jnp.repeat(jnp.exp(draws), shape[dim] // shards_of).reshape((-1,) + (1,) * (len(shape) - dim - 1))

    level = one(*shards[0])
    for cut in shards[1:]:
        level = level * one(*cut)
    return level


def centred(own_key, shape, deviation, bound, shards=(), kind=jnp.bfloat16):
    array = deviation * jax.random.normal(own_key, shape, jnp.float32)
    if shards:
        array = array * steps_of(own_key, shape, shards, -0.22, 0.18)
    return jnp.clip(array, -bound, bound).astype(kind)


def setup_inputs(seed: int = 0) -> dict:
    arg_keys = jax.random.split(jax.random.key(seed), 5)
    inverse_factor = draw_inverse_factor(jax.random.fold_in(arg_keys[4], 71), 0)
    coupling = centred(arg_keys[1], (SUBS, FEMDOF, BROWS), 0.03, 0.19921875, ((0, 32),))
    boundary_tiles = draw_boundary_tiles(jax.random.fold_in(arg_keys[4], 71), 0)
    bem_block = draw_bem_block(jax.random.fold_in(arg_keys[4], 71), 0)
    return dict(inverse_factor=inverse_factor, coupling=coupling, boundary_tiles=boundary_tiles, bem_block=bem_block)


def factor(square):
    extent = square.shape[0]
    if extent <= 16:
        for column in range(extent - 1):
            scaled = square[column + 1:, column] / square[column, column]
            square = square.at[column + 1:, column].set(scaled)
            square = square.at[column + 1:, column + 1:].add(-scaled[:, None] * square[column, column + 1:][None, :])
        return square
    halfway = extent // 2
    leading = factor(square[:halfway, :halfway])
    lower_part = jnp.tril(leading, -1) + jnp.eye(halfway, dtype=square.dtype)
    upper_part = jnp.triu(leading)
    right_part = jax.scipy.linalg.solve_triangular(lower_part, square[:halfway, halfway:], lower=True, unit_diagonal=True)
    below_part = jax.scipy.linalg.solve_triangular(upper_part, square[halfway:, :halfway].T, trans=1, lower=False).T
    remainder = factor(square[halfway:, halfway:] - jnp.dot(below_part, right_part, precision=lax.Precision.HIGHEST))
    top_half = jnp.concatenate([leading, right_part], axis=1)
    bottom_half = jnp.concatenate([below_part, remainder], axis=1)
    return jnp.concatenate([top_half, bottom_half], axis=0)

def reference(inverse_factor, coupling, boundary_tiles, bem_block):
    offsets = jnp.arange(TILE, dtype=jnp.int32)
    residue = (jnp.arange(SUBS, dtype=jnp.int32) // N_COL % N_ROW).astype(jnp.int32)

    def accumulate(carried, inputs):
        factor_sub, coupling_sub, tiles_sub, residue_sub = inputs
        coupled = jnp.dot(factor_sub.astype(jnp.float32), coupling_sub.astype(jnp.float32), preferred_element_type=jnp.float32).astype(jnp.bfloat16)
        rounded = jnp.dot(coupled.T.astype(jnp.float32), coupled.astype(jnp.float32), preferred_element_type=jnp.float32).astype(jnp.bfloat16)
        contribution = lax.optimization_barrier(rounded).astype(jnp.float32)
        indices = ((N_ROW * tiles_sub + residue_sub)[:, None] * TILE + offsets[None, :]).reshape(-1).astype(jnp.int32)
        carried = carried.at[indices[:, None], indices[None, :]].add(contribution)
        return (carried, None)
    assembled, _ = lax.scan(accumulate, jnp.zeros((NB, NB), jnp.float32), (inverse_factor, coupling, boundary_tiles, residue))
    boundary = bem_block.reshape(NB, NB) + assembled
    for panel in range(PANELS):
        start_col = panel * PW
        stop_col = start_col + PW
        packed = factor(boundary[start_col:stop_col, start_col:stop_col])
        lower_unit = jnp.tril(packed, -1) + jnp.eye(PW, dtype=packed.dtype)
        upper_part = jnp.triu(packed)
        upper_rows = jax.scipy.linalg.solve_triangular(lower_unit, boundary[start_col:stop_col, stop_col:], lower=True, unit_diagonal=True)
        lower_rows = jax.scipy.linalg.solve_triangular(upper_part, boundary[stop_col:, start_col:stop_col].T, trans=1, lower=False).T
        update = jnp.dot(lower_rows, upper_rows, precision=lax.Precision.HIGHEST)
        boundary = boundary.at[stop_col:, stop_col:].set(boundary[stop_col:, stop_col:] - update)
        boundary = boundary.at[start_col:stop_col, stop_col:].set(upper_rows)
        boundary = boundary.at[stop_col:, start_col:stop_col].set(lower_rows)
        boundary = boundary.at[start_col:stop_col, start_col:stop_col].set(packed)
    return boundary.reshape(bem_block.shape)
```

```python
import functools

import jax
import jax.numpy as jnp
from jax import lax
from jax.experimental import pallas as pl
from jax.experimental.pallas import tpu as pltpu
from jax.sharding import PartitionSpec as P

PW = 256


def broadcast(value, axis, root):
    mine = lax.axis_index(axis) == root
    return lax.psum(jnp.where(mine, value, jnp.zeros_like(value)), axis)


def highest(left, right):
    return jnp.dot(left, right, precision=lax.Precision.HIGHEST)


BASE = 64

def dotp(a, b):
    return jnp.dot(a, b, precision=lax.Precision.HIGHEST, preferred_element_type=jnp.float32)

def eliminate_base(block, base):
    sub = lax.broadcasted_iota(jnp.int32, (8, 2 * base), 0)
    lane = lax.broadcasted_iota(jnp.int32, (8, 2 * base), 1)
    groups = base // 8
    m = []
    for v in range(groups):
        rows = block[8 * v:8 * v + 8, :]
        unit = jnp.where(lane == sub + (base + 8 * v), 1.0, 0.0).astype(jnp.float32)
        wide = jnp.concatenate([rows, jnp.zeros((8, base), jnp.float32)], axis=1)
        m.append(wide + unit)
    for v in range(groups):
        m.append(jnp.where(lane == sub + 8 * v, 1.0, 0.0).astype(jnp.float32))
    for j in range(base):
        g, r = divmod(j, 8)
        pivot_rows = m[g]
        row = jnp.broadcast_to(pivot_rows[r:r + 1, :], (8, 2 * base))
        pivot = jnp.broadcast_to(row[:, j:j + 1], (8, 2 * base))
        inv = 1.0 / pivot
        scaled = jnp.where(lane > j, row * inv, 0.0)
        for v in list(range(g, groups)) + list(range(groups, groups + g + 1)):
            col = jnp.broadcast_to(m[v][:, j:j + 1], (8, 2 * base))
            put = lane == j
            if v == g:
                col = jnp.where(sub > r, col, 0.0)
                put = put & (sub > r)
            m[v] = jnp.where(put, col * inv, m[v] - col * scaled)
    packed = jnp.concatenate([m[v][:, :base] for v in range(groups)], axis=0)
    lower = jnp.concatenate([m[v][:, base:] for v in range(groups)], axis=0)
    upper = jnp.concatenate([m[v][:, :base] for v in range(groups, 2 * groups)], axis=0)
    return packed, lower, upper

def factor_kernel(n, base, square_ref, packed_ref, lower_ref, upper_ref, w):
    total = 2 * n
    w[:n, :n] = square_ref[...]
    eye = (lax.broadcasted_iota(jnp.int32, (n, n), 0) == lax.broadcasted_iota(jnp.int32, (n, n), 1)).astype(jnp.float32)
    w[:n, n:] = eye
    w[n:, :n] = eye
    w[n:, n:] = jnp.zeros((n, n), jnp.float32)
    rest = total - base
    rows = lax.broadcasted_iota(jnp.int32, (rest, base), 0)
    lanes = lax.broadcasted_iota(jnp.int32, (base, rest), 1)

    def step(b, carry):
        live = rest - b * base
        full = w[...]
        packed, lower, upper = eliminate_base(full[:base, :base], base)
        right = full[:base, base:]
        below = full[base:, :base]
        right_new = dotp(lower, right)
        below_new = dotp(below, upper)
        right_live = jnp.where(lanes < live, right_new, 0.0)
        below_live = jnp.where(rows < live, below_new, 0.0)
        trail = full[base:, base:] - dotp(below_live, right_live)
        right_keep = jnp.where(lanes < live, right_new, right)
        below_keep = jnp.where(rows < live, below_new, below)
        w[:rest, :] = jnp.concatenate([trail, below_keep], axis=1)
        w[rest:, :] = jnp.concatenate([right_keep, packed], axis=1)
        return carry

    lax.fori_loop(0, n // base, step, 0)
    packed_ref[...] = w[n:, n:]
    lower_ref[...] = w[n:, :n]
    upper_ref[...] = w[:n, n:]

def factor(square):
    n = square.shape[0]
    shape = jax.ShapeDtypeStruct((n, n), jnp.float32)
    return pl.pallas_call(
        functools.partial(factor_kernel, n, BASE),
        out_shape=(shape, shape, shape),
        scratch_shapes=[pltpu.VMEM((2 * n, 2 * n), jnp.float32)],
        compiler_params=pltpu.CompilerParams(vmem_limit_bytes=48 << 20),
        name="factor",
    )(square)


def local(inverse_factor, coupling, boundary_tiles, bem_block):
    fem_count = lax.axis_size("fem")
    row_count = lax.axis_size("row")
    col_count = lax.axis_size("col")
    fem_index = lax.axis_index("fem")
    row_index = lax.axis_index("row")
    col_index = lax.axis_index("col")
    row_tiles = bem_block.shape[0]
    tile_size = bem_block.shape[2]
    local_width = bem_block.shape[3]
    slot_count = boundary_tiles.shape[1]
    class_tiles = row_tiles * fem_count
    per_block = class_tiles // col_count
    coupled = jnp.dot(inverse_factor[0], coupling[0], preferred_element_type=jnp.float32).astype(
        jnp.bfloat16
    )
    schur = lax.dot_general(
        coupled, coupled, (((0,), (0,)), ((), ())), preferred_element_type=jnp.float32
    ).astype(jnp.bfloat16)
    subdomain = (fem_index * row_count + row_index) * col_count + col_index
    chosen = lax.dynamic_index_in_dim(boundary_tiles, subdomain, 0, keepdims=False)
    one_hot = (chosen[None, :] == jnp.arange(class_tiles, dtype=jnp.int32)[:, None]).astype(
        jnp.bfloat16
    )
    row_pick = one_hot.reshape(row_tiles, fem_count, slot_count)
    col_pick = one_hot.reshape(col_count, per_block, slot_count)
    blocks = schur.reshape(slot_count, tile_size, slot_count, tile_size)
    by_rows = jnp.einsum("kga,aibj->gkibj", row_pick, blocks, preferred_element_type=jnp.bfloat16)
    placed = jnp.einsum("cmb,gkibj->gckimj", col_pick, by_rows, preferred_element_type=jnp.bfloat16)
    block_width = per_block * tile_size
    placed = placed.reshape(fem_count * col_count, row_tiles, tile_size, block_width)
    received = lax.all_to_all(placed, ("fem", "col"), split_axis=0, concat_axis=0, tiled=True)
    summed = jnp.sum(received, axis=0, dtype=jnp.float32)
    residue_mask = (jnp.arange(row_count) == row_index).astype(jnp.float32)
    spread = (
        summed.reshape(row_tiles, tile_size, per_block, 1, tile_size)
        * residue_mask[None, None, None, :, None]
    )
    matrix = bem_block[:, 0] + spread.reshape(row_tiles, tile_size, local_width)
    device = fem_index * row_count + row_index
    class_count = fem_count * row_count
    global_rows = (
        (jnp.arange(row_tiles)[:, None] * class_count + device) * tile_size
        + jnp.arange(tile_size)[None, :]
    ).reshape(-1)
    global_cols = col_index * local_width + jnp.arange(local_width)
    panel_tiles = PW // tile_size
    stop_col = PW
    pieces = [
        broadcast(matrix[0], ("fem", "row"), 0 * panel_tiles + member)
        for member in range(panel_tiles)
    ]
    panel_top = jnp.concatenate(pieces, axis=0)
    flattened = matrix.reshape(row_tiles * tile_size, local_width)
    diagonal = jnp.where(col_index == 0, panel_top[:, 0:stop_col], jnp.eye(PW, dtype=jnp.float32))
    packed, lower_inv, upper_inv = factor(diagonal)
    panel_cols = jnp.where(col_index == 0, flattened[:, 0:stop_col], 0.0)
    lower_rows = highest(panel_cols, upper_inv)
    packed, lower_inv, lower_rows = (
        broadcast(packed, "col", 0),
        broadcast(lower_inv, "col", 0),
        broadcast(lower_rows, "col", 0),
    )
    upper_rows = highest(lower_inv, panel_top)
    update = highest(lower_rows, upper_rows)
    below_mask = global_rows >= stop_col
    right_mask = global_cols >= stop_col
    rows_inside = (global_rows >= 0) & (global_rows < stop_col)
    cols_inside = (global_cols >= 0) & (global_cols < stop_col)
    lower_full = jnp.zeros(flattened.shape, jnp.float32).at[:, 0:stop_col].set(lower_rows)
    upper_full = jnp.where(col_index == 0, upper_rows.at[:, 0:stop_col].set(packed), upper_rows)
    gathered = upper_full[jnp.clip(global_rows - 0, 0, PW - 1)]
    result = jnp.where(below_mask[:, None] & right_mask[None, :], flattened - update, flattened)
    result = jnp.where(below_mask[:, None] & cols_inside[None, :], lower_full, result)
    result = jnp.where(rows_inside[:, None] & (global_cols >= 0)[None, :], gathered, result)
    matrix = result.reshape(row_tiles, tile_size, local_width)
    return matrix[:, None]


def solution(mesh):
    placed = (
        P(("fem", "row", "col"), None, None),
        P(("fem", "row", "col"), None, None),
        P(),
        P(None, ("fem", "row"), None, "col"),
    )
    return jax.shard_map(
        local,
        mesh=mesh,
        in_specs=placed,
        out_specs=P(None, ("fem", "row"), None, "col"),
        check_vma=False,
    )
```

```python
import functools

import jax
import jax.numpy as jnp
from jax import lax
from jax.experimental import pallas as pl
from jax.experimental.pallas import tpu as pltpu
from jax.sharding import PartitionSpec as P

PW = 256


def broadcast(value, axis, root):
    mine = lax.axis_index(axis) == root
    return lax.psum(jnp.where(mine, value, jnp.zeros_like(value)), axis)


def highest(left, right):
    return jnp.dot(left, right, precision=lax.Precision.HIGHEST)


BASE = 64

def dotp(a, b):
    return jnp.dot(a, b, precision=lax.Precision.HIGHEST, preferred_element_type=jnp.float32)

def eliminate_base(block, base):
    sub = lax.broadcasted_iota(jnp.int32, (8, 2 * base), 0)
    lane = lax.broadcasted_iota(jnp.int32, (8, 2 * base), 1)
    groups = base // 8
    m = []
    for v in range(groups):
        rows = block[8 * v:8 * v + 8, :]
        unit = jnp.where(lane == sub + (base + 8 * v), 1.0, 0.0).astype(jnp.float32)
        wide = jnp.concatenate([rows, jnp.zeros((8, base), jnp.float32)], axis=1)
        m.append(wide + unit)
    for v in range(groups):
        m.append(jnp.where(lane == sub + 8 * v, 1.0, 0.0).astype(jnp.float32))
    for j in range(base):
        g, r = divmod(j, 8)
        pivot_rows = m[g]
        row = jnp.broadcast_to(pivot_rows[r:r + 1, :], (8, 2 * base))
        pivot = jnp.broadcast_to(row[:, j:j + 1], (8, 2 * base))
        inv = 1.0 / pivot
        scaled = jnp.where(lane > j, row * inv, 0.0)
        for v in list(range(g, groups)) + list(range(groups, groups + g + 1)):
            col = jnp.broadcast_to(m[v][:, j:j + 1], (8, 2 * base))
            put = lane == j
            if v == g:
                col = jnp.where(sub > r, col, 0.0)
                put = put & (sub > r)
            m[v] = jnp.where(put, col * inv, m[v] - col * scaled)
    packed = jnp.concatenate([m[v][:, :base] for v in range(groups)], axis=0)
    lower = jnp.concatenate([m[v][:, base:] for v in range(groups)], axis=0)
    upper = jnp.concatenate([m[v][:, :base] for v in range(groups, 2 * groups)], axis=0)
    return packed, lower, upper

def factor_kernel(n, base, square_ref, packed_ref, lower_ref, upper_ref, w):
    total = 2 * n
    w[:n, :n] = square_ref[...]
    eye = (lax.broadcasted_iota(jnp.int32, (n, n), 0) == lax.broadcasted_iota(jnp.int32, (n, n), 1)).astype(jnp.float32)
    w[:n, n:] = eye
    w[n:, :n] = eye
    w[n:, n:] = jnp.zeros((n, n), jnp.float32)
    rest = total - base
    rows = lax.broadcasted_iota(jnp.int32, (rest, base), 0)
    lanes = lax.broadcasted_iota(jnp.int32, (base, rest), 1)

    def step(b, carry):
        live = rest - b * base
        full = w[...]
        packed, lower, upper = eliminate_base(full[:base, :base], base)
        right = full[:base, base:]
        below = full[base:, :base]
        right_new = dotp(lower, right)
        below_new = dotp(below, upper)
        right_live = jnp.where(lanes < live, right_new, 0.0)
        below_live = jnp.where(rows < live, below_new, 0.0)
        trail = full[base:, base:] - dotp(below_live, right_live)
        right_keep = jnp.where(lanes < live, right_new, right)
        below_keep = jnp.where(rows < live, below_new, below)
        w[:rest, :] = jnp.concatenate([trail, below_keep], axis=1)
        w[rest:, :] = jnp.concatenate([right_keep, packed], axis=1)
        return carry

    lax.fori_loop(0, n // base, step, 0)
    packed_ref[...] = w[n:, n:]
    lower_ref[...] = w[n:, :n]
    upper_ref[...] = w[:n, n:]

def factor(square):
    n = square.shape[0]
    shape = jax.ShapeDtypeStruct((n, n), jnp.float32)
    return pl.pallas_call(
        functools.partial(factor_kernel, n, BASE),
        out_shape=(shape, shape, shape),
        scratch_shapes=[pltpu.VMEM((2 * n, 2 * n), jnp.float32)],
        compiler_params=pltpu.CompilerParams(vmem_limit_bytes=48 << 20),
        name="factor",
    )(square)


def local(inverse_factor, coupling, boundary_tiles, bem_block):
    fem_count = lax.axis_size("fem")
    row_count = lax.axis_size("row")
    col_count = lax.axis_size("col")
    fem_index = lax.axis_index("fem")
    row_index = lax.axis_index("row")
    col_index = lax.axis_index("col")
    row_tiles = bem_block.shape[0]
    tile_size = bem_block.shape[2]
    local_width = bem_block.shape[3]
    slot_count = boundary_tiles.shape[1]
    class_tiles = row_tiles * fem_count
    per_block = class_tiles // col_count
    coupled = jnp.dot(inverse_factor[0], coupling[0], preferred_element_type=jnp.float32).astype(
        jnp.bfloat16
    )
    schur = lax.dot_general(
        coupled, coupled, (((0,), (0,)), ((), ())), preferred_element_type=jnp.float32
    ).astype(jnp.bfloat16)
    subdomain = (fem_index * row_count + row_index) * col_count + col_index
    chosen = lax.dynamic_index_in_dim(boundary_tiles, subdomain, 0, keepdims=False)
    one_hot = (chosen[None, :] == jnp.arange(class_tiles, dtype=jnp.int32)[:, None]).astype(
        jnp.bfloat16
    )
    row_pick = one_hot.reshape(row_tiles, fem_count, slot_count)
    col_pick = one_hot.reshape(col_count, per_block, slot_count)
    blocks = schur.reshape(slot_count, tile_size, slot_count, tile_size)
    by_rows = jnp.einsum("kga,aibj->gkibj", row_pick, blocks, preferred_element_type=jnp.bfloat16)
    placed = jnp.einsum("cmb,gkibj->gckimj", col_pick, by_rows, preferred_element_type=jnp.bfloat16)
    block_width = per_block * tile_size
    placed = placed.reshape(fem_count * col_count, row_tiles, tile_size, block_width)
    received = lax.all_to_all(placed, ("fem", "col"), split_axis=0, concat_axis=0, tiled=True)
    summed = jnp.sum(received, axis=0, dtype=jnp.float32)
    residue_mask = (jnp.arange(row_count) == row_index).astype(jnp.float32)
    spread = (
        summed.reshape(row_tiles, tile_size, per_block, 1, tile_size)
        * residue_mask[None, None, None, :, None]
    )
    matrix = bem_block[:, 0] + spread.reshape(row_tiles, tile_size, local_width)
    device = fem_index * row_count + row_index
    class_count = fem_count * row_count
    global_rows = (
        (jnp.arange(row_tiles)[:, None] * class_count + device) * tile_size
        + jnp.arange(tile_size)[None, :]
    ).reshape(-1)
    global_cols = col_index * local_width + jnp.arange(local_width)
    panel_tiles = PW // tile_size
    stop_col = PW
    pieces = [
        broadcast(matrix[0], ("fem", "row"), 0 * panel_tiles + member)
        for member in range(panel_tiles)
    ]
    panel_top = jnp.concatenate(pieces, axis=0)
    flattened = matrix.reshape(row_tiles * tile_size, local_width)
    diagonal = jnp.where(col_index == 0, panel_top[:, 0:stop_col], jnp.eye(PW, dtype=jnp.float32))
    packed, lower_inv, upper_inv = factor(diagonal)
    panel_cols = jnp.where(col_index == 0, flattened[:, 0:stop_col], 0.0)
    lower_rows = highest(panel_cols, upper_inv)
    packed, lower_inv, lower_rows = (
        broadcast(packed, "col", 0),
        broadcast(lower_inv, "col", 0),
        broadcast(lower_rows, "col", 0),
    )
    upper_rows = highest(lower_inv, panel_top)
    update = highest(lower_rows, upper_rows)
    below_mask = global_rows >= stop_col
    right_mask = global_cols >= stop_col
    rows_inside = (global_rows >= 0) & (global_rows < stop_col)
    cols_inside = (global_cols >= 0) & (global_cols < stop_col)
    lower_full = jnp.zeros(flattened.shape, jnp.float32).at[:, 0:stop_col].set(lower_rows)
    upper_full = jnp.where(col_index == 0, upper_rows.at[:, 0:stop_col].set(packed), upper_rows)
    gathered = upper_full[jnp.clip(global_rows - 0, 0, PW - 1)]
    result = jnp.where(below_mask[:, None] & right_mask[None, :], flattened - update, flattened)
    result = jnp.where(below_mask[:, None] & cols_inside[None, :], lower_full, result)
    result = jnp.where(rows_inside[:, None] & (global_cols >= 0)[None, :], gathered, result)
    matrix = result.reshape(row_tiles, tile_size, local_width)
    return matrix[:, None]


def pair_table(slots):
    pairs = [(a, a) for a in range(slots)]
    pairs += [(a, b) for a in range(slots) for b in range(a + 1, slots)]
    return {pair: place for place, pair in enumerate(pairs)}


def schur_kernel(slots, tile, block, zero_ref, left_hbm, right_hbm, first_ref, second_ref, diag_ref,
                 left, right, product, flipped, left_sems, right_sems):
    order = left.shape[0]
    table = pair_table(slots)
    half = first_ref.shape[0]
    steps = order // block
    wide = block // tile

    def left_copy(i):
        window = (pl.ds(i * block, block), pl.ds(0, (i + 1) * block))
        return pltpu.make_async_copy(left_hbm.at[window], left.at[window], left_sems.at[i])

    def right_copy(i):
        window = pl.ds(i * block, block)
        return pltpu.make_async_copy(right_hbm.at[window], right.at[window], right_sems.at[i])

    for i in range(steps):
        right_copy(i).start()
        left_copy(i).start()
    for i in range(steps):
        right_copy(i).wait()
        left_copy(i).wait()
        reach = (i + 1) * block
        rows = jnp.dot(left[i * block:reach, :reach], right[:reach, :],
                       preferred_element_type=jnp.float32).astype(jnp.bfloat16)
        product[i * block:reach, :] = rows
        flipped[:, i * block:reach] = rows.T
    for j in range(slots // wide):
        tall = (j + 1) * block
        part = jnp.dot(flipped[:tall, :], product[:, j * block:tall],
                       preferred_element_type=jnp.float32).astype(jnp.bfloat16)
        for b in range(j * wide, (j + 1) * wide):
            for a in range(b + 1):
                value = part[a * tile:(a + 1) * tile, (b - j * wide) * tile:(b - j * wide + 1) * tile]
                place = table[a, b]
                if place < half:
                    first_ref[place] = value
                else:
                    second_ref[place - half] = value
    slot = zero_ref[0]
    value = first_ref[jnp.maximum(slot, 0)].astype(jnp.float32)
    diag_ref[...] = jnp.where(slot >= 0, value, 0.0)


def schur(zero, inverse_factor, coupling, slots, tile):
    order, width = coupling.shape
    count = len(pair_table(slots))
    half = count // 2
    block = 2 * tile
    steps = order // block
    halves = jax.ShapeDtypeStruct((half, tile, tile), jnp.bfloat16)
    return pl.pallas_call(
        functools.partial(schur_kernel, slots, tile, block),
        out_shape=(halves, jax.ShapeDtypeStruct((count - half, tile, tile), jnp.bfloat16),
                   jax.ShapeDtypeStruct((tile, tile), jnp.float32)),
        in_specs=[pl.BlockSpec(memory_space=pltpu.SMEM), pl.BlockSpec(memory_space=pl.ANY),
                  pl.BlockSpec(memory_space=pl.ANY)],
        out_specs=(pl.BlockSpec(memory_space=pltpu.VMEM),) * 3,
        scratch_shapes=[pltpu.VMEM((order, order), jnp.bfloat16), pltpu.VMEM((order, width), jnp.bfloat16),
                        pltpu.VMEM((order, width), jnp.bfloat16), pltpu.VMEM((width, order), jnp.bfloat16),
                        pltpu.SemaphoreType.DMA((steps,)), pltpu.SemaphoreType.DMA((steps,))],
        compiler_params=pltpu.CompilerParams(vmem_limit_bytes=40 << 20),
        name="schur",
    )(zero, inverse_factor, coupling)


def visit(slots, tiles_ref, place_ref, packs, eye, fem_count, fem, wanted, add):
    for source, (first, second) in enumerate(packs):
        half = first.shape[0]

        def rows(a, carry, source=source, first=first, second=second, half=half):
            row_tile = tiles_ref[source * slots + a]

            @pl.when(lax.rem(row_tile, fem_count) == fem)
            def _():
                def columns(b, inner):
                    col_tile = tiles_ref[source * slots + b]

                    @pl.when(wanted(row_tile, col_tile))
                    def _():
                        place = place_ref[a * slots + b]
                        for ref, base in ((first, 0), (second, half)):
                            inside = (place >= base) & (place < base + ref.shape[0])

                            @pl.when(inside & (a <= b))
                            def _():
                                add(row_tile, col_tile, ref[place - base].astype(jnp.float32))

                            @pl.when(inside & (a > b))
                            def _():
                                add(row_tile, col_tile,
                                    lax.dot_general(eye, ref[place - base], (((1,), (1,)), ((), ())),
                                                    preferred_element_type=jnp.float32))
                    return inner
                return_value = lax.fori_loop(0, slots, columns, 0)
                del return_value
            return carry

        lax.fori_loop(0, slots, rows, 0)


def tile_eye(tile):
    return (lax.broadcasted_iota(jnp.int32, (tile, tile), 0)
            == lax.broadcasted_iota(jnp.int32, (tile, tile), 1)).astype(jnp.bfloat16)


def cross_kernel(slots, fem_count, per_block, tiles_ref, place_ref, here_ref, *refs):
    packs = [(refs[2 * i], refs[2 * i + 1]) for i in range(4)]
    out_ref, strip_ref, strip_send_ref, total = refs[8:]
    tile = out_ref.shape[-1]
    eye = tile_eye(tile)
    fem, target = here_ref[0], here_ref[2]
    total[...] = jnp.zeros_like(total)
    strip_ref[...] = jnp.zeros_like(strip_ref)

    def add(row_tile, col_tile, value):
        @pl.when(lax.div(col_tile, per_block) == target)
        def _():
            k, m = lax.div(row_tile, fem_count), lax.rem(col_tile, per_block)
            total[k, m] += value

        @pl.when(col_tile == 0)
        def _():
            strip_ref[lax.div(row_tile, fem_count)] += value

    visit(slots, tiles_ref, place_ref, packs, eye, fem_count, fem,
          lambda r, c: (lax.div(c, per_block) == target) | (c == 0), add)
    out_ref[...] = total[...].astype(jnp.bfloat16)
    strip_send_ref[...] = strip_ref[...].astype(jnp.bfloat16)


def own_kernel(slots, fem_count, per_block, tiles_ref, place_ref, here_ref, *refs):
    packs = [(refs[2 * i], refs[2 * i + 1]) for i in range(4)]
    out_ref = refs[8]
    eye = tile_eye(out_ref.shape[-1])
    fem, target = here_ref[0], here_ref[1]
    out_ref[...] = jnp.zeros_like(out_ref)

    def add(row_tile, col_tile, value):
        k, m = lax.div(row_tile, fem_count), lax.rem(col_tile, per_block)
        out_ref[k, m] += value

    visit(slots, tiles_ref, place_ref, packs, eye, fem_count, fem,
          lambda r, c: lax.div(c, per_block) == target, add)


def call_visit(kernel, name, outs, scratch, tiles, place, here, packs):
    vmem = pl.BlockSpec(memory_space=pltpu.VMEM)
    smem = pl.BlockSpec(memory_space=pltpu.SMEM)
    flat = [half for pack in packs for half in pack]
    return pl.pallas_call(
        kernel,
        out_shape=outs,
        in_specs=[smem] * 3 + [vmem] * len(flat),
        out_specs=tuple(vmem for _ in outs),
        scratch_shapes=scratch,
        compiler_params=pltpu.CompilerParams(vmem_limit_bytes=32 << 20),
        name=name,
    )(tiles, place, here, *flat)


def split(value):
    high = value.astype(jnp.bfloat16)
    return high, (value - high.astype(jnp.float32)).astype(jnp.bfloat16)


def three_pass(left, right):
    (left_high, left_low), (right_high, right_low) = left, right

    def product(a, b):
        return jnp.dot(a, b, preferred_element_type=jnp.float32)

    return product(left_high, right_high) + (product(left_high, right_low) + product(left_low, right_high))


def panel_kernel(per_block, row_count, here_ref, lower_ref, upper_ref, mine_ref, other_ref, mine_strip_ref,
                 other_strip_ref, left_ref, strip_ref, strip_other_ref, upper_rows_ref, lower_rows_ref, top, cols):
    row = here_ref[3]
    tile = mine_ref.shape[0]
    odd = lax.rem(row, 2)
    for member, (rows_ref, extra_ref) in ((0, (mine_ref, mine_strip_ref)), (1, (other_ref, other_strip_ref))):
        residue = odd if member == 0 else 1 - odd
        base = pl.multiple_of(residue * tile, tile)
        top[pl.ds(base, tile), :] = rows_ref[...]
        for m in range(per_block):
            lanes = pl.ds(pl.multiple_of((m * row_count + residue) * tile, tile), tile)
            top[pl.ds(base, tile), lanes] += extra_ref[m]
    count = left_ref.shape[0]
    for k in range(count):
        cols[k * tile:(k + 1) * tile, :] = left_ref[k]

    @pl.when(row < 2)
    def _():
        lanes = pl.ds(pl.multiple_of(odd * tile, tile), tile)
        for k in range(count):
            cols[k * tile:(k + 1) * tile, lanes] += strip_ref[k] + strip_other_ref[k].astype(jnp.float32)

    lower = split(lower_ref[...])
    step = 2 * upper_ref.shape[0]
    for i in range(top.shape[1] // step):
        upper_rows_ref[:, i * step:(i + 1) * step] = three_pass(lower, split(top[:, i * step:(i + 1) * step]))
    upper = split(upper_ref[...])
    for i in range(cols.shape[0] // step):
        lower_rows_ref[i * step:(i + 1) * step, :] = three_pass(split(cols[i * step:(i + 1) * step, :]), upper)


def panel(here, lower, upper, mine, other, mine_strip, other_strip, left, strip, strip_other, per_block, row_count):
    n = lower.shape[0]
    count, tile, _ = left.shape
    width = mine.shape[1]
    vmem = pl.BlockSpec(memory_space=pltpu.VMEM)
    return pl.pallas_call(
        functools.partial(panel_kernel, per_block, row_count),
        out_shape=(jax.ShapeDtypeStruct((n, width), jnp.float32),
                   jax.ShapeDtypeStruct((count * tile, n), jnp.float32)),
        in_specs=[pl.BlockSpec(memory_space=pltpu.SMEM)] + [vmem] * 9,
        out_specs=(vmem, vmem),
        scratch_shapes=[pltpu.VMEM((n, width), jnp.float32), pltpu.VMEM((count * tile, n), jnp.float32)],
        compiler_params=pltpu.CompilerParams(vmem_limit_bytes=40 << 20),
        name="panel",
    )(here, lower, upper, mine, other, mine_strip, other_strip, left, strip, strip_other)


def finish_kernel(row_count, fem_count, here_ref, bem_ref, own_ref, recv_ref, lower_ref, upper_ref, packed_ref,
                  out_ref, lower_high, lower_low):
    step = pl.program_id(0)
    fem, col, row = here_ref[0], here_ref[1], here_ref[3]
    device = fem * row_count + row
    count, _, tile, width = bem_ref.shape

    @pl.when(step == 0)
    def _():
        high, low = split(lower_ref[...])
        lower_high[...] = high
        lower_low[...] = low

    corner = (col == 0) & (step == 0)

    @pl.when(jnp.logical_not(corner))
    def _():
        update = three_pass((lower_high[...], lower_low[...]), split(upper_ref[...]))
        for k in range(count):
            out_ref[k, 0] = bem_ref[k, 0] - update[k * tile:(k + 1) * tile, :]

        @pl.when(lax.div(row, 2) == lax.rem(step, 2))
        def _():
            lanes = pl.ds(pl.multiple_of(lax.rem(row, 2) * tile, tile), tile)
            for k in range(count):
                out_ref[k, 0, :, lanes] += own_ref[k, 0] + recv_ref[k, 0].astype(jnp.float32)

        @pl.when(device < 2)
        def _():
            out_ref[0, 0] = upper_ref[pl.ds(pl.multiple_of(device * tile, tile), tile), :]

    @pl.when(corner)
    def _():
        for k in range(count):
            out_ref[k, 0] = lower_ref[k * tile:(k + 1) * tile, :]

        @pl.when(device < 2)
        def _():
            out_ref[0, 0] = packed_ref[pl.ds(pl.multiple_of(device * tile, tile), tile), :]


def finish(here, bem_block, own, recv, lower_rows, upper_rows, packed, row_count, fem_count):
    count, _, tile, width = bem_block.shape
    n = packed.shape[0]
    tiles_wide = n // tile
    whole = lambda shape: pl.BlockSpec(shape, lambda i: (0,) * len(shape))
    contribution = pl.BlockSpec((count, 1, tile, tile), lambda i: (0, i * tiles_wide // row_count, 0, 0))
    wide = pl.BlockSpec((count, 1, tile, n), lambda i: (0, 0, 0, i))
    return pl.pallas_call(
        functools.partial(finish_kernel, row_count, fem_count),
        grid=(width // n,),
        out_shape=jax.ShapeDtypeStruct(bem_block.shape, jnp.float32),
        in_specs=[pl.BlockSpec(memory_space=pltpu.SMEM), wide, contribution, contribution,
                  whole(lower_rows.shape), pl.BlockSpec((n, n), lambda i: (0, i)), whole(packed.shape)],
        out_specs=wide,
        scratch_shapes=[pltpu.VMEM(lower_rows.shape, jnp.bfloat16), pltpu.VMEM(lower_rows.shape, jnp.bfloat16)],
        compiler_params=pltpu.CompilerParams(vmem_limit_bytes=40 << 20),
        name="finish",
    )(here, bem_block, own, recv, lower_rows, upper_rows, packed)


def local_square(inverse_factor, coupling, boundary_tiles, bem_block):
    fem_count = lax.axis_size("fem")
    row_count = lax.axis_size("row")
    col_count = lax.axis_size("col")
    fem, row, col = lax.axis_index("fem"), lax.axis_index("row"), lax.axis_index("col")
    count, _, tile, width = bem_block.shape
    slots = boundary_tiles.shape[1]
    class_tiles = count * fem_count
    per_block = class_tiles // col_count
    swap_fem = [(0, 1), (1, 0)]
    swap_near = [(0, 1), (1, 0), (2, 3), (3, 2)]
    swap_far = [(0, 2), (1, 3), (2, 0), (3, 1)]
    near = lambda v: lax.ppermute(v, "col", swap_near)
    far = lambda v: lax.ppermute(v, "col", swap_far)
    across = lambda v: lax.ppermute(v, "fem", swap_fem)
    core = lambda v: lax.ppermute(v, "row", swap_near)
    over = lambda v: lax.ppermute(v, "row", [(0, 2), (1, 3)])

    def tiles_of(f, c):
        return lax.dynamic_index_in_dim(boundary_tiles, (f * row_count + row) * col_count + c, 0, keepdims=False)

    mine = tiles_of(fem, col)
    near_col = col + 1 - 2 * (col % 2)
    far_col = (col + 2) % 4
    tiles = jnp.concatenate([mine, tiles_of(1 - fem, col), tiles_of(fem, near_col), tiles_of(1 - fem, near_col)])
    table = pair_table(slots)
    place = jnp.asarray([table[min(a, b), max(a, b)] for a in range(slots) for b in range(slots)], jnp.int32)
    here = jnp.stack([fem, col, far_col, row]).astype(jnp.int32)
    zero = jnp.max(jnp.where(mine == 0, jnp.arange(slots, dtype=jnp.int32), -1)).reshape(1)

    left = bem_block[:, 0, :, :PW]
    for step in range(col_count - 1):
        left = jnp.where(col == step + 1, lax.ppermute(left, "col", [(step, step + 1)]), left)
    rows = bem_block[0, 0]
    rows = jnp.where(fem == 1, lax.ppermute(rows, "fem", [(0, 1)]), rows)
    rows = jnp.where(row >= 2, over(rows), rows)
    rows_other = core(rows)

    first, second, diag = schur(zero, inverse_factor[0], coupling[0], slots, tile)

    corner = jnp.where((fem == 0) & (col == 0), bem_block[0, 0, :, :PW], 0.0)
    lane_tile = jnp.arange(PW) // tile
    corner = corner + jnp.where(lane_tile == row, jnp.tile(diag, (1, PW // tile)), 0.0)
    corner = corner + across(corner)
    corner = corner + near(corner)
    corner = corner + far(corner)
    corner = jnp.where(row >= 2, over(corner), corner)
    corner_other = core(corner)
    odd = row % 2 == 1
    square = jnp.concatenate([jnp.where(odd, corner_other, corner), jnp.where(odd, corner, corner_other)], axis=0)
    packed, lower_inv, upper_inv = factor(square)

    first_f, second_f, first_n, second_n = across(first), across(second), near(first), near(second)
    first_fn = near(first_f)
    second_fn = across(second_n)
    packs = [(first, second), (first_f, second_f), (first_n, second_n), (first_fn, second_fn)]
    block = (count, per_block, tile, tile)
    cross, strip, strip_send = call_visit(
        functools.partial(cross_kernel, slots, fem_count, per_block), "cross",
        (jax.ShapeDtypeStruct(block, jnp.bfloat16), jax.ShapeDtypeStruct((count, tile, tile), jnp.float32),
         jax.ShapeDtypeStruct((count, tile, tile), jnp.bfloat16)),
        [pltpu.VMEM(block, jnp.float32)], tiles, place, here, packs)
    strip_other = far(strip_send)
    recv = far(cross)
    own, = call_visit(functools.partial(own_kernel, slots, fem_count, per_block), "own",
                      (jax.ShapeDtypeStruct(block, jnp.float32),), [], tiles, place, here, packs)

    share = per_block // fem_count
    local_strip = (lax.dynamic_slice_in_dim(strip, col * share, share, 0)
                   + lax.dynamic_slice_in_dim(strip_other, col * share, share, 0).astype(jnp.float32))
    local_strip = jnp.swapaxes(local_strip, 1, 2)
    turned = across(local_strip)
    even = jnp.where(fem == 0, local_strip, turned)
    other = jnp.where(fem == 0, turned, local_strip)
    top_strip = jnp.stack([even, other], axis=1).reshape(per_block, tile, tile)
    top_strip = jnp.where(row >= 2, over(top_strip), top_strip)
    top_other = core(top_strip)
    upper_rows, lower_rows = panel(here, lower_inv, upper_inv, rows, rows_other, top_strip, top_other, left,
                                   strip, strip_other, per_block, row_count)
    return finish(here, bem_block, own, recv, lower_rows, upper_rows, packed, row_count, fem_count)


def solution(mesh):
    placed = (
        P(("fem", "row", "col"), None, None),
        P(("fem", "row", "col"), None, None),
        P(),
        P(None, ("fem", "row"), None, "col"),
    )
    sizes = dict(mesh.shape)
    square = sizes["fem"] == 2 and sizes["row"] == 4 and sizes["col"] == 4
    return jax.shard_map(
        local_square if square else local,
        mesh=mesh,
        in_specs=placed,
        out_specs=P(None, ("fem", "row"), None, "col"),
        check_vma=False,
    )
```

```python
import functools

import jax
import jax.numpy as jnp
from jax import lax
from jax.experimental import pallas as pl
from jax.experimental.pallas import tpu as pltpu
from jax.sharding import PartitionSpec as P

PW = 256
SHARE = 1


def broadcast(value, axis, root):
    mine = lax.axis_index(axis) == root
    return lax.psum(jnp.where(mine, value, jnp.zeros_like(value)), axis)


def highest(left, right):
    return jnp.dot(left, right, precision=lax.Precision.HIGHEST)


BASE = 64

def dotp(a, b):
    return jnp.dot(a, b, precision=lax.Precision.HIGHEST, preferred_element_type=jnp.float32)

def eliminate_base(block, base):
    sub = lax.broadcasted_iota(jnp.int32, (8, 2 * base), 0)
    lane = lax.broadcasted_iota(jnp.int32, (8, 2 * base), 1)
    groups = base // 8
    m = []
    for v in range(groups):
        rows = block[8 * v:8 * v + 8, :]
        unit = jnp.where(lane == sub + (base + 8 * v), 1.0, 0.0).astype(jnp.float32)
        wide = jnp.concatenate([rows, jnp.zeros((8, base), jnp.float32)], axis=1)
        m.append(wide + unit)
    for v in range(groups):
        m.append(jnp.where(lane == sub + 8 * v, 1.0, 0.0).astype(jnp.float32))
    for j in range(base):
        g, r = divmod(j, 8)
        pivot_rows = m[g]
        row = jnp.broadcast_to(pivot_rows[r:r + 1, :], (8, 2 * base))
        pivot = jnp.broadcast_to(row[:, j:j + 1], (8, 2 * base))
        inv = 1.0 / pivot
        scaled = jnp.where(lane > j, row * inv, 0.0)
        for v in list(range(g, groups)) + list(range(groups, groups + g + 1)):
            col = jnp.broadcast_to(m[v][:, j:j + 1], (8, 2 * base))
            put = lane == j
            if v == g:
                col = jnp.where(sub > r, col, 0.0)
                put = put & (sub > r)
            m[v] = jnp.where(put, col * inv, m[v] - col * scaled)
    packed = jnp.concatenate([m[v][:, :base] for v in range(groups)], axis=0)
    lower = jnp.concatenate([m[v][:, base:] for v in range(groups)], axis=0)
    upper = jnp.concatenate([m[v][:, :base] for v in range(groups, 2 * groups)], axis=0)
    return packed, lower, upper

def factor_steps(n, base, w, steps):
    total = 2 * n
    rest = total - base
    rows = lax.broadcasted_iota(jnp.int32, (rest, base), 0)
    lanes = lax.broadcasted_iota(jnp.int32, (base, rest), 1)

    def step(b, carry):
        live = rest - b * base
        full = w[...]
        packed, lower, upper = eliminate_base(full[:base, :base], base)
        right = full[:base, base:]
        below = full[base:, :base]
        right_new = dotp(lower, right)
        below_new = dotp(below, upper)
        right_live = jnp.where(lanes < live, right_new, 0.0)
        below_live = jnp.where(rows < live, below_new, 0.0)
        trail = full[base:, base:] - dotp(below_live, right_live)
        right_keep = jnp.where(lanes < live, right_new, right)
        below_keep = jnp.where(rows < live, below_new, below)
        w[:rest, :] = jnp.concatenate([trail, below_keep], axis=1)
        w[rest:, :] = jnp.concatenate([right_keep, packed], axis=1)
        return carry

    lax.fori_loop(steps[0], steps[1], step, 0)


def factor_kernel(n, base, steps, first, last, *refs):
    if first:
        square_ref, w = refs[0], refs[-1]
        eye = (lax.broadcasted_iota(jnp.int32, (n, n), 0)
               == lax.broadcasted_iota(jnp.int32, (n, n), 1)).astype(jnp.float32)
        w[:n, :n] = square_ref[...]
        w[:n, n:] = eye
        w[n:, :n] = eye
        w[n:, n:] = jnp.zeros((n, n), jnp.float32)
    else:
        state_ref, w = refs[0], refs[-1]
        w[...] = state_ref[...]
    factor_steps(n, base, w, steps)
    if last:
        packed_ref, lower_ref, upper_ref = refs[1:4]
        packed_ref[...] = w[n:, n:]
        lower_ref[...] = w[n:, :n]
        upper_ref[...] = w[:n, n:]


def factor_call(value, n, steps, first, last):
    square = jax.ShapeDtypeStruct((n, n), jnp.float32)
    wide = jax.ShapeDtypeStruct((2 * n, 2 * n), jnp.float32)
    return pl.pallas_call(
        functools.partial(factor_kernel, n, BASE, steps, first, last),
        out_shape=(square,) * 3 if last else wide,
        scratch_shapes=[pltpu.VMEM((2 * n, 2 * n), jnp.float32)] if last else [],
        compiler_params=pltpu.CompilerParams(vmem_limit_bytes=32 << 20),
        name="factor",
    )(value)


def factor(square):
    n = square.shape[0]
    return factor_call(square, n, (0, n // BASE), True, True)


def factor_half(square):
    n = square.shape[0]
    return factor_call(square, n, (0, n // BASE // 2), True, False)


def factor_rest(state):
    n = state.shape[0] // 2
    return factor_call(state, n, (n // BASE // 2, n // BASE), False, True)


def after(value, *others):
    return lax.optimization_barrier((value, *others))[0]


def local(inverse_factor, coupling, boundary_tiles, bem_block):
    fem_count = lax.axis_size("fem")
    row_count = lax.axis_size("row")
    col_count = lax.axis_size("col")
    fem_index = lax.axis_index("fem")
    row_index = lax.axis_index("row")
    col_index = lax.axis_index("col")
    row_tiles = bem_block.shape[0]
    tile_size = bem_block.shape[2]
    local_width = bem_block.shape[3]
    slot_count = boundary_tiles.shape[1]
    class_tiles = row_tiles * fem_count
    per_block = class_tiles // col_count
    coupled = jnp.dot(inverse_factor[0], coupling[0], preferred_element_type=jnp.float32).astype(
        jnp.bfloat16
    )
    schur = lax.dot_general(
        coupled, coupled, (((0,), (0,)), ((), ())), preferred_element_type=jnp.float32
    ).astype(jnp.bfloat16)
    subdomain = (fem_index * row_count + row_index) * col_count + col_index
    chosen = lax.dynamic_index_in_dim(boundary_tiles, subdomain, 0, keepdims=False)
    one_hot = (chosen[None, :] == jnp.arange(class_tiles, dtype=jnp.int32)[:, None]).astype(
        jnp.bfloat16
    )
    row_pick = one_hot.reshape(row_tiles, fem_count, slot_count)
    col_pick = one_hot.reshape(col_count, per_block, slot_count)
    blocks = schur.reshape(slot_count, tile_size, slot_count, tile_size)
    by_rows = jnp.einsum("kga,aibj->gkibj", row_pick, blocks, preferred_element_type=jnp.bfloat16)
    placed = jnp.einsum("cmb,gkibj->gckimj", col_pick, by_rows, preferred_element_type=jnp.bfloat16)
    block_width = per_block * tile_size
    placed = placed.reshape(fem_count * col_count, row_tiles, tile_size, block_width)
    received = lax.all_to_all(placed, ("fem", "col"), split_axis=0, concat_axis=0, tiled=True)
    summed = jnp.sum(received, axis=0, dtype=jnp.float32)
    residue_mask = (jnp.arange(row_count) == row_index).astype(jnp.float32)
    spread = (
        summed.reshape(row_tiles, tile_size, per_block, 1, tile_size)
        * residue_mask[None, None, None, :, None]
    )
    matrix = bem_block[:, 0] + spread.reshape(row_tiles, tile_size, local_width)
    device = fem_index * row_count + row_index
    class_count = fem_count * row_count
    global_rows = (
        (jnp.arange(row_tiles)[:, None] * class_count + device) * tile_size
        + jnp.arange(tile_size)[None, :]
    ).reshape(-1)
    global_cols = col_index * local_width + jnp.arange(local_width)
    panel_tiles = PW // tile_size
    stop_col = PW
    pieces = [
        broadcast(matrix[0], ("fem", "row"), 0 * panel_tiles + member)
        for member in range(panel_tiles)
    ]
    panel_top = jnp.concatenate(pieces, axis=0)
    flattened = matrix.reshape(row_tiles * tile_size, local_width)
    diagonal = jnp.where(col_index == 0, panel_top[:, 0:stop_col], jnp.eye(PW, dtype=jnp.float32))
    packed, lower_inv, upper_inv = factor(diagonal)
    panel_cols = jnp.where(col_index == 0, flattened[:, 0:stop_col], 0.0)
    lower_rows = highest(panel_cols, upper_inv)
    packed, lower_inv, lower_rows = (
        broadcast(packed, "col", 0),
        broadcast(lower_inv, "col", 0),
        broadcast(lower_rows, "col", 0),
    )
    upper_rows = highest(lower_inv, panel_top)
    update = highest(lower_rows, upper_rows)
    below_mask = global_rows >= stop_col
    right_mask = global_cols >= stop_col
    rows_inside = (global_rows >= 0) & (global_rows < stop_col)
    cols_inside = (global_cols >= 0) & (global_cols < stop_col)
    lower_full = jnp.zeros(flattened.shape, jnp.float32).at[:, 0:stop_col].set(lower_rows)
    upper_full = jnp.where(col_index == 0, upper_rows.at[:, 0:stop_col].set(packed), upper_rows)
    gathered = upper_full[jnp.clip(global_rows - 0, 0, PW - 1)]
    result = jnp.where(below_mask[:, None] & right_mask[None, :], flattened - update, flattened)
    result = jnp.where(below_mask[:, None] & cols_inside[None, :], lower_full, result)
    result = jnp.where(rows_inside[:, None] & (global_cols >= 0)[None, :], gathered, result)
    matrix = result.reshape(row_tiles, tile_size, local_width)
    return matrix[:, None]


def pair_table(slots):
    pairs = [(a, a) for a in range(slots)]
    pairs += [(a, b) for a in range(slots) for b in range(a + 1, slots)]
    return {pair: place for place, pair in enumerate(pairs)}


def schur_kernel(slots, tile, block, zero_ref, left_hbm, right_hbm, first_ref, second_ref, diag_ref, token_ref,
                 left, right, product, flipped, left_sems, right_sems):
    order = left.shape[0]
    table = pair_table(slots)
    half = first_ref.shape[0]
    steps = order // block
    wide = block // tile

    def left_copy(i):
        window = (pl.ds(i * block, block), pl.ds(0, (i + 1) * block))
        return pltpu.make_async_copy(left_hbm.at[window], left.at[window], left_sems.at[i])

    def right_copy(i):
        window = pl.ds(i * block, block)
        return pltpu.make_async_copy(right_hbm.at[window], right.at[window], right_sems.at[i])

    for i in range(steps):
        right_copy(i).start()
        left_copy(i).start()
    for i in range(steps):
        right_copy(i).wait()
        left_copy(i).wait()
        reach = (i + 1) * block
        rows = jnp.dot(left[i * block:reach, :reach], right[:reach, :],
                       preferred_element_type=jnp.float32).astype(jnp.bfloat16)
        product[i * block:reach, :] = rows
        flipped[:, i * block:reach] = rows.T
    for j in range(slots // wide):
        tall = (j + 1) * block
        part = jnp.dot(flipped[:tall, :], product[:, j * block:tall],
                       preferred_element_type=jnp.float32).astype(jnp.bfloat16)
        for b in range(j * wide, (j + 1) * wide):
            for a in range(b + 1):
                value = part[a * tile:(a + 1) * tile, (b - j * wide) * tile:(b - j * wide + 1) * tile]
                place = table[a, b]
                if place < half:
                    first_ref[place] = value
                else:
                    second_ref[place - half] = value
    slot = zero_ref[0]
    value = first_ref[jnp.maximum(slot, 0)].astype(jnp.float32)
    diag_ref[...] = jnp.where(slot >= 0, value, 0.0)
    token_ref[0] = 0


def schur(zero, inverse_factor, coupling, slots, tile):
    order, width = coupling.shape
    count = len(pair_table(slots))
    half = count * SHARE // 4
    block = 2 * tile
    steps = order // block
    halves = jax.ShapeDtypeStruct((half, tile, tile), jnp.bfloat16)
    return pl.pallas_call(
        functools.partial(schur_kernel, slots, tile, block),
        out_shape=(halves, jax.ShapeDtypeStruct((count - half, tile, tile), jnp.bfloat16),
                   jax.ShapeDtypeStruct((tile, tile), jnp.float32), jax.ShapeDtypeStruct((1,), jnp.int32)),
        in_specs=[pl.BlockSpec(memory_space=pltpu.SMEM), pl.BlockSpec(memory_space=pltpu.HBM),
                  pl.BlockSpec(memory_space=pltpu.HBM)],
        out_specs=(pl.BlockSpec(memory_space=pltpu.VMEM),) * 3 + (pl.BlockSpec(memory_space=pltpu.SMEM),),
        scratch_shapes=[pltpu.VMEM((order, order), jnp.bfloat16), pltpu.VMEM((order, width), jnp.bfloat16),
                        pltpu.VMEM((order, width), jnp.bfloat16), pltpu.VMEM((width, order), jnp.bfloat16),
                        pltpu.SemaphoreType.DMA((steps,)), pltpu.SemaphoreType.DMA((steps,))],
        compiler_params=pltpu.CompilerParams(vmem_limit_bytes=40 << 20),
        name="schur",
    )(zero, inverse_factor, coupling)


def pick_table(tiles, rows, columns, slots):
    sources = tiles.shape[0]
    count = slots * (slots + 1) // 2

    def slot_of(wanted):
        hit = tiles[None, :, :] == wanted[:, None, None]
        return jnp.max(jnp.where(hit, jnp.arange(slots, dtype=jnp.int32), -1), axis=2)

    a = slot_of(rows)[:, None, :]
    b = slot_of(columns)[None, :, :]
    low, high = jnp.minimum(a, b), jnp.maximum(a, b)
    place = jnp.where(a == b, a, slots + low * (2 * slots - 1 - low) // 2 + high - low - 1)
    place = place + count * jnp.arange(sources, dtype=jnp.int32)
    there = low >= 0
    empty = count * sources
    direct = jnp.where(there & (a <= b), place, empty)
    turned = jnp.where(there & (a > b), place, empty)
    return jnp.stack([direct, turned], axis=2).astype(jnp.int32)


def collect_kernel(sources, lists, table_refs, packs, outs, store, sems):
    count = (store.shape[0] - 1) // sources
    copies = []
    for source in range(sources):
        base = source * count
        for half in range(2):
            ref = packs[2 * source + half]
            size = ref.shape[0]
            copies.append(pltpu.make_async_copy(ref, store.at[pl.ds(base, size)], sems.at[2 * source + half]))
            base += size
    for copy in copies:
        copy.start()
    store[count * sources] = jnp.zeros(store.shape[1:], store.dtype)
    for copy in copies:
        copy.wait()
    for (rows, columns), table, group in zip(lists, table_refs, outs):
        def one(i, carry, columns=columns, table=table, group=group):
            k, m = lax.div(i, columns), lax.rem(i, columns)
            base = i * 2 * sources
            direct = store[table[base]].astype(jnp.float32)
            turned = store[table[base + sources]].astype(jnp.float32)
            for source in range(1, sources):
                direct = direct + store[table[base + source]].astype(jnp.float32)
                turned = turned + store[table[base + sources + source]].astype(jnp.float32)
            total = direct + turned.T
            for ref in group:
                ref[k, m] = total.astype(ref.dtype)
            return carry

        lax.fori_loop(0, rows * columns, one, 0, unroll=2)


def collect(name, tables, packs, types):
    sources = len(packs)
    flat = [half for pack in packs for half in pack]
    tile = flat[0].shape[-1]
    count = packs[0][0].shape[0] + packs[0][1].shape[0]
    lists = [table.shape[:2] for table in tables]
    shapes = [jax.ShapeDtypeStruct((*dims, tile, tile), kind) for dims, kinds in zip(lists, types) for kind in kinds]

    def kernel(*refs):
        table_refs, refs = refs[:len(tables)], refs[len(tables):]
        pack_refs, refs = refs[:len(flat)], refs[len(flat):]
        groups = []
        for kinds in types:
            groups.append(refs[:len(kinds)])
            refs = refs[len(kinds):]
        store, sems = refs
        collect_kernel(sources, lists, table_refs, pack_refs, groups, store, sems)

    vmem = pl.BlockSpec(memory_space=pltpu.VMEM)
    return pl.pallas_call(
        kernel,
        out_shape=tuple(shapes),
        in_specs=[pl.BlockSpec(memory_space=pltpu.SMEM)] * len(tables)
        + [pl.BlockSpec(memory_space=pl.ANY)] * len(flat),
        out_specs=tuple(vmem for _ in shapes),
        scratch_shapes=[pltpu.VMEM((count * sources + 1, tile, tile), jnp.bfloat16),
                        pltpu.SemaphoreType.DMA((len(flat),))],
        compiler_params=pltpu.CompilerParams(vmem_limit_bytes=24 << 20),
        name=name,
    )(*[table.reshape(-1) for table in tables], *flat)


def split(value):
    high = value.astype(jnp.bfloat16)
    return high, (value - high.astype(jnp.float32)).astype(jnp.bfloat16)


def three_pass(left, right):
    (left_high, left_low), (right_high, right_low) = left, right

    def product(a, b):
        return jnp.dot(a, b, preferred_element_type=jnp.float32)

    return product(left_high, right_high) + (product(left_high, right_low) + product(left_low, right_high))


def panel_kernel(per_block, row_count, here_ref, lower_ref, upper_ref, mine_ref, other_ref, mine_strip_ref,
                 other_strip_ref, strip_ref, *refs):
    lefts, (upper_rows_ref, lower_rows_ref, top, cols, sems) = refs[:-5], refs[-5:]
    col, row = here_ref[1], here_ref[3]
    tile = mine_ref.shape[0]
    count = strip_ref.shape[0]
    n = lower_ref.shape[0]

    def take(k, source):
        return pltpu.make_async_copy(source.at[k], cols.at[pl.ds(k * tile, tile)], sems.at[k])

    for place, source in enumerate(lefts):
        @pl.when(col == place)
        def _():
            for k in range(count):
                take(k, source).start()
    odd = lax.rem(row, 2)
    for member, (rows_ref, extra_ref) in ((0, (mine_ref, mine_strip_ref)), (1, (other_ref, other_strip_ref))):
        residue = odd if member == 0 else 1 - odd
        base = pl.multiple_of(residue * tile, tile)
        top[pl.ds(base, tile), :] = rows_ref[...]
        for m in range(per_block):
            lanes = pl.ds(pl.multiple_of((m * row_count + residue) * tile, tile), tile)
            top[pl.ds(base, tile), lanes] += extra_ref[m]
    lower = split(lower_ref[...])
    step = 2 * n
    for i in range(top.shape[1] // step):
        upper_rows_ref[:, i * step:(i + 1) * step] = three_pass(lower, split(top[:, i * step:(i + 1) * step]))
    for k in range(count):
        take(k, lefts[0]).wait()

    @pl.when(row < 2)
    def _():
        lanes = pl.ds(pl.multiple_of(odd * tile, tile), tile)
        for k in range(count):
            cols[k * tile:(k + 1) * tile, lanes] += strip_ref[k]

    upper = split(upper_ref[...])
    for i in range(cols.shape[0] // step):
        high, low = split(three_pass(split(cols[i * step:(i + 1) * step, :]), upper))
        lower_rows_ref[i * step:(i + 1) * step, :n] = high
        lower_rows_ref[i * step:(i + 1) * step, n:] = low


def panel(here, lower, upper, mine, other, mine_strip, other_strip, strip, lefts, per_block, row_count):
    n = lower.shape[0]
    count, tile, _ = lefts[0].shape
    width = mine.shape[1]
    vmem = pl.BlockSpec(memory_space=pltpu.VMEM)
    return pl.pallas_call(
        functools.partial(panel_kernel, per_block, row_count),
        out_shape=(jax.ShapeDtypeStruct((n, width), jnp.float32),
                   jax.ShapeDtypeStruct((count * tile, 2 * n), jnp.bfloat16)),
        in_specs=[pl.BlockSpec(memory_space=pltpu.SMEM)] + [vmem] * 7
        + [pl.BlockSpec(memory_space=pltpu.HBM)] * len(lefts),
        out_specs=(vmem, vmem),
        scratch_shapes=[pltpu.VMEM((n, width), jnp.float32), pltpu.VMEM((count * tile, n), jnp.float32),
                        pltpu.SemaphoreType.DMA((count,))],
        compiler_params=pltpu.CompilerParams(vmem_limit_bytes=40 << 20),
        name="panel",
    )(here, lower, upper, mine, other, mine_strip, other_strip, strip, *lefts)


def finish_kernel(row_count, here_ref, bem_ref, own_ref, recv_ref, lower_ref, upper_ref, packed_ref, out_ref):
    step = pl.program_id(0)
    fem, col, row = here_ref[0], here_ref[1], here_ref[3]
    device = fem * row_count + row
    count, _, tile, n = bem_ref.shape
    corner = (col == 0) & (step == 0)

    @pl.when(jnp.logical_not(corner))
    def _():
        high, low = split(upper_ref[...])
        both = jnp.dot(lower_ref[...], jnp.concatenate([high, high], axis=0), preferred_element_type=jnp.float32)
        update = both + jnp.dot(lower_ref[:, :n], low, preferred_element_type=jnp.float32)
        for k in range(count):
            out_ref[k, 0] = bem_ref[k, 0] - update[k * tile:(k + 1) * tile, :]

        @pl.when(lax.div(row, 2) == lax.rem(step, 2))
        def _():
            lanes = pl.ds(pl.multiple_of(lax.rem(row, 2) * tile, tile), tile)
            for k in range(count):
                out_ref[k, 0, :, lanes] += own_ref[k, 0] + recv_ref[k, 0].astype(jnp.float32)

        @pl.when(device < 2)
        def _():
            out_ref[0, 0] = upper_ref[pl.ds(pl.multiple_of(device * tile, tile), tile), :]

    @pl.when(corner)
    def _():
        for k in range(count):
            rows = slice(k * tile, (k + 1) * tile)
            out_ref[k, 0] = lower_ref[rows, :n].astype(jnp.float32) + lower_ref[rows, n:].astype(jnp.float32)

        @pl.when(device < 2)
        def _():
            out_ref[0, 0] = packed_ref[pl.ds(pl.multiple_of(device * tile, tile), tile), :]


def finish(here, bem_block, own, recv, lower_rows, upper_rows, packed, row_count):
    count, _, tile, width = bem_block.shape
    n = packed.shape[0]
    tiles_wide = n // tile
    whole = lambda shape: pl.BlockSpec(shape, lambda i: (0,) * len(shape))
    contribution = pl.BlockSpec((count, 1, tile, tile), lambda i: (0, i * tiles_wide // row_count, 0, 0))
    wide = pl.BlockSpec((count, 1, tile, n), lambda i: (0, 0, 0, i))
    return pl.pallas_call(
        functools.partial(finish_kernel, row_count),
        grid=(width // n,),
        out_shape=jax.ShapeDtypeStruct(bem_block.shape, jnp.float32),
        in_specs=[pl.BlockSpec(memory_space=pltpu.SMEM), wide, contribution, contribution,
                  whole(lower_rows.shape), pl.BlockSpec((n, n), lambda i: (0, i)), whole(packed.shape)],
        out_specs=wide,
        compiler_params=pltpu.CompilerParams(vmem_limit_bytes=40 << 20),
        name="finish",
    )(here, bem_block, own, recv, lower_rows, upper_rows, packed)


def local_square(inverse_factor, coupling, boundary_tiles, bem_block):
    fem_count = lax.axis_size("fem")
    row_count = lax.axis_size("row")
    col_count = lax.axis_size("col")
    fem, row, col = lax.axis_index("fem"), lax.axis_index("row"), lax.axis_index("col")
    count, _, tile, width = bem_block.shape
    slots = boundary_tiles.shape[1]
    class_tiles = count * fem_count
    per_block = class_tiles // col_count
    swap_fem = [(0, 1), (1, 0)]
    swap_near = [(0, 1), (1, 0), (2, 3), (3, 2)]
    swap_far = [(0, 2), (1, 3), (2, 0), (3, 1)]
    near = lambda v: lax.ppermute(v, "col", swap_near)
    far = lambda v: lax.ppermute(v, "col", swap_far)
    across = lambda v: lax.ppermute(v, "fem", swap_fem)
    core = lambda v: lax.ppermute(v, "row", swap_near)
    over = lambda v: lax.ppermute(v, "row", [(0, 2), (1, 3)])

    def tiles_of(f, c):
        return lax.dynamic_index_in_dim(boundary_tiles, (f * row_count + row) * col_count + c, 0, keepdims=False)

    mine = tiles_of(fem, col)
    near_col = col + 1 - 2 * (col % 2)
    far_col = (col + 2) % 4
    tiles = jnp.stack([mine, tiles_of(1 - fem, col), tiles_of(fem, near_col), tiles_of(1 - fem, near_col)])
    here = jnp.stack([fem, col, far_col, row]).astype(jnp.int32)
    zero = jnp.max(jnp.where(mine == 0, jnp.arange(slots, dtype=jnp.int32), -1)).reshape(1)
    held = jnp.arange(count, dtype=jnp.int32) * fem_count + fem
    block_cols = jnp.arange(per_block, dtype=jnp.int32)
    share = per_block // fem_count
    far_table = pick_table(tiles, held, far_col * per_block + block_cols, slots)
    own_table = pick_table(tiles, held, col * per_block + block_cols, slots)
    strip_table = pick_table(tiles, held, jnp.zeros((1,), jnp.int32), slots)

    lefts = [bem_block[:, 0, :, :PW]]
    lefts.append(lax.ppermute(lefts[0], "col", [(0, 1)]))

    first, second, diag, token = schur(zero, inverse_factor[0], coupling[0], slots, tile)

    second_n, first_f, first_n, second_f = near(second), across(first), near(first), across(second)
    first_fn = near(first_f)
    second_fn = across(second_n)
    packs = [(first, second), (first_f, second_f), (first_n, second_n), (first_fn, second_fn)]

    rows = lax.dynamic_slice(bem_block, (token[0], 0, 0, 0), (1, 1, tile, width))[0, 0]
    rows_over = over(rows)

    corner = jnp.where((fem == 0) & (col == 0), bem_block[0, 0, :, :PW], 0.0)
    lane_tile = jnp.arange(PW) // tile
    corner = corner + jnp.where(lane_tile == row, jnp.tile(diag, (1, PW // tile)), 0.0)
    corner = corner + across(corner)
    corner = corner + near(corner)
    corner = corner + far(corner)
    corner = jnp.where(row >= 2, over(corner), corner)
    corner_other = core(corner)
    odd = row % 2 == 1
    square = jnp.concatenate([jnp.where(odd, corner_other, corner), jnp.where(odd, corner, corner_other)], axis=0)
    lefts.append(lax.ppermute(lefts[1], "col", [(1, 2)]))
    state = factor_half(square)

    far_table = after(far_table, state)
    cross, strip, strip_send = collect("cross", [far_table, strip_table], packs,
                                       [(jnp.bfloat16,), (jnp.float32, jnp.bfloat16)])
    strip, strip_send = strip[:, 0], strip_send[:, 0]
    recv = far(cross)
    part = count // 2
    start = (col % 2) * part
    strip_half = (lax.dynamic_slice_in_dim(strip, start, part, 0)
                  + far(lax.dynamic_slice_in_dim(strip_send, start, part, 0)).astype(jnp.float32))
    rows_all = after(jnp.where(row >= 2, rows_over, rows), cross)
    rows_all = jnp.where(fem == 1, lax.ppermute(rows_all, "fem", [(0, 1)]), rows_all)
    lefts.append(lax.ppermute(after(lefts[2], cross), "col", [(2, 3)]))
    own_table = after(own_table, cross)
    own, = collect("own", [own_table], packs, [(jnp.float32,)])
    packed, lower_inv, upper_inv = factor_rest(after(state, own))

    strip_half = after(strip_half, packed)
    strip_near = near(strip_half)
    low = col % 2 == 0
    strip = jnp.concatenate([jnp.where(low, strip_half, strip_near), jnp.where(low, strip_near, strip_half)], axis=0)
    rows_other = core(rows_all)

    local_strip = jnp.swapaxes(lax.dynamic_slice_in_dim(strip, col * share, share, 0), 1, 2)
    turned = across(local_strip)
    even = jnp.where(fem == 0, local_strip, turned)
    other = jnp.where(fem == 0, turned, local_strip)
    top_strip = jnp.stack([even, other], axis=1).reshape(per_block, tile, tile)
    top_strip = jnp.where(row >= 2, over(top_strip), top_strip)
    top_other = core(top_strip)
    upper_rows, lower_rows = panel(here, lower_inv, upper_inv, rows_all, rows_other, top_strip, top_other, strip,
                                   lefts, per_block, row_count)
    return finish(here, bem_block, own, recv, lower_rows, upper_rows, packed, row_count)


def solution(mesh):
    placed = (
        P(("fem", "row", "col"), None, None),
        P(("fem", "row", "col"), None, None),
        P(),
        P(None, ("fem", "row"), None, "col"),
    )
    sizes = dict(mesh.shape)
    square = sizes["fem"] == 2 and sizes["row"] == 4 and sizes["col"] == 4
    return jax.shard_map(
        local_square if square else local,
        mesh=mesh,
        in_specs=placed,
        out_specs=P(None, ("fem", "row"), None, "col"),
        check_vma=False,
    )
```

```python
import functools

import jax
import jax.numpy as jnp
from jax import lax
from jax.experimental import pallas as pl
from jax.experimental.pallas import tpu as pltpu
from jax.sharding import PartitionSpec as P


PW = 256
SHARE = 0.4


def broadcast(value, axis, root):
    mine = lax.axis_index(axis) == root
    return lax.psum(jnp.where(mine, value, jnp.zeros_like(value)), axis)


def highest(left, right):
    return jnp.dot(left, right, precision=lax.Precision.HIGHEST)


BASE = 64


def dotp(a, b):
    return jnp.dot(a, b, precision=lax.Precision.HIGHEST, preferred_element_type=jnp.float32)


def eliminate_base(block, base):
    shape = (8, 2 * base)
    sub = lax.broadcasted_iota(jnp.int32, shape, 0)
    lane = lax.broadcasted_iota(jnp.int32, shape, 1)
    groups = base // 8

    def row_of(value, i):
        return jnp.broadcast_to(value[i:i + 1, :], shape)

    def columns_of(value, first):
        return [jnp.broadcast_to(value[:, first + i:first + i + 1], shape) for i in range(8)]

    m = []
    for v in range(groups):
        unit = jnp.where(lane == sub + (base + 8 * v), 1.0, 0.0).astype(jnp.float32)
        wide = jnp.concatenate([block[8 * v:8 * v + 8, :], jnp.zeros((8, base), jnp.float32)], axis=1)
        m.append(wide + unit)
    for v in range(groups):
        m.append(jnp.where(lane == sub + 8 * v, 1.0, 0.0).astype(jnp.float32))
    for g in range(groups):
        first = 8 * g
        live = lane >= first
        current = m[g]
        held = columns_of(current, first)
        inverses, rows, upper, factors = [], [], {}, []
        for i in range(8):
            inverse = 1.0 / row_of(held[i], i)
            factor_i = jnp.where(sub > i, held[i] * inverse, 0.0)
            for k in range(i + 1, 8):
                upper[i, k] = row_of(held[k], i)
                held[k] = held[k] - factor_i * upper[i, k]
            row = jnp.where(live, row_of(current, i), 0.0)
            current = current - factor_i * row
            inverses.append(inverse)
            rows.append(row)
            factors.append(factor_i)
        for i in range(8):
            current = jnp.where((lane == first + i) & (sub > i), factors[i], current)
        m[g] = current
        for v in list(range(g + 1, groups)) + list(range(groups, groups + g + 1)):
            held = columns_of(m[v], first)
            current = m[v]
            for i in range(8):
                factor_i = held[i] * inverses[i]
                for k in range(i + 1, 8):
                    held[k] = held[k] - factor_i * upper[i, k]
                current = current - factor_i * rows[i]
                held[i] = factor_i
            for i in range(8):
                current = jnp.where(lane == first + i, held[i], current)
            m[v] = current
    packed = jnp.concatenate([m[v][:, :base] for v in range(groups)], axis=0)
    lower = jnp.concatenate([m[v][:, base:] for v in range(groups)], axis=0)
    upper = jnp.concatenate([m[v][:, :base] for v in range(groups, 2 * groups)], axis=0)
    return packed, lower, upper


def factor_steps(n, base, w, steps):
    total = 2 * n
    rest = total - base
    rows = lax.broadcasted_iota(jnp.int32, (rest, base), 0)
    lanes = lax.broadcasted_iota(jnp.int32, (base, rest), 1)

    def step(b, carry):
        live = rest - b * base
        full = w[...]
        packed, lower, upper = eliminate_base(full[:base, :base], base)
        right = full[:base, base:]
        below = full[base:, :base]
        right_new = dotp(lower, right)
        below_new = dotp(below, upper)
        right_live = jnp.where(lanes < live, right_new, 0.0)
        below_live = jnp.where(rows < live, below_new, 0.0)
        trail = full[base:, base:] - dotp(below_live, right_live)
        right_keep = jnp.where(lanes < live, right_new, right)
        below_keep = jnp.where(rows < live, below_new, below)
        w[:rest, :] = jnp.concatenate([trail, below_keep], axis=1)
        w[rest:, :] = jnp.concatenate([right_keep, packed], axis=1)
        return carry

    lax.fori_loop(steps[0], steps[1], step, 0)


def factor_kernel(n, base, square_ref, packed_ref, lower_ref, upper_ref, w):
    eye = (lax.broadcasted_iota(jnp.int32, (n, n), 0)
           == lax.broadcasted_iota(jnp.int32, (n, n), 1)).astype(jnp.float32)
    w[:n, :n] = square_ref[...]
    w[:n, n:] = eye
    w[n:, :n] = eye
    w[n:, n:] = jnp.zeros((n, n), jnp.float32)
    factor_steps(n, base, w, (0, n // base))
    packed_ref[...] = w[n:, n:]
    lower_ref[...] = w[n:, :n]
    upper_ref[...] = w[:n, n:]


def factor(square):
    n = square.shape[0]
    shape = jax.ShapeDtypeStruct((n, n), jnp.float32)
    return pl.pallas_call(
        functools.partial(factor_kernel, n, BASE),
        out_shape=(shape,) * 3,
        scratch_shapes=[pltpu.VMEM((2 * n, 2 * n), jnp.float32)],
        compiler_params=pltpu.CompilerParams(vmem_limit_bytes=32 << 20),
        name="factor",
    )(square)


def after(value, *others):
    return lax.optimization_barrier((value, *others))[0]


def local(inverse_factor, coupling, boundary_tiles, bem_block):
    fem_count = lax.axis_size("fem")
    row_count = lax.axis_size("row")
    col_count = lax.axis_size("col")
    fem_index = lax.axis_index("fem")
    row_index = lax.axis_index("row")
    col_index = lax.axis_index("col")
    row_tiles = bem_block.shape[0]
    tile_size = bem_block.shape[2]
    local_width = bem_block.shape[3]
    slot_count = boundary_tiles.shape[1]
    class_tiles = row_tiles * fem_count
    per_block = class_tiles // col_count
    coupled = jnp.dot(inverse_factor[0], coupling[0], preferred_element_type=jnp.float32).astype(
        jnp.bfloat16
    )
    schur = lax.dot_general(
        coupled, coupled, (((0,), (0,)), ((), ())), preferred_element_type=jnp.float32
    ).astype(jnp.bfloat16)
    subdomain = (fem_index * row_count + row_index) * col_count + col_index
    chosen = lax.dynamic_index_in_dim(boundary_tiles, subdomain, 0, keepdims=False)
    one_hot = (chosen[None, :] == jnp.arange(class_tiles, dtype=jnp.int32)[:, None]).astype(
        jnp.bfloat16
    )
    row_pick = one_hot.reshape(row_tiles, fem_count, slot_count)
    col_pick = one_hot.reshape(col_count, per_block, slot_count)
    blocks = schur.reshape(slot_count, tile_size, slot_count, tile_size)
    by_rows = jnp.einsum("kga,aibj->gkibj", row_pick, blocks, preferred_element_type=jnp.bfloat16)
    placed = jnp.einsum("cmb,gkibj->gckimj", col_pick, by_rows, preferred_element_type=jnp.bfloat16)
    block_width = per_block * tile_size
    placed = placed.reshape(fem_count * col_count, row_tiles, tile_size, block_width)
    received = lax.all_to_all(placed, ("fem", "col"), split_axis=0, concat_axis=0, tiled=True)
    summed = jnp.sum(received, axis=0, dtype=jnp.float32)
    residue_mask = (jnp.arange(row_count) == row_index).astype(jnp.float32)
    spread = (
        summed.reshape(row_tiles, tile_size, per_block, 1, tile_size)
        * residue_mask[None, None, None, :, None]
    )
    matrix = bem_block[:, 0] + spread.reshape(row_tiles, tile_size, local_width)
    device = fem_index * row_count + row_index
    class_count = fem_count * row_count
    global_rows = (
        (jnp.arange(row_tiles)[:, None] * class_count + device) * tile_size
        + jnp.arange(tile_size)[None, :]
    ).reshape(-1)
    global_cols = col_index * local_width + jnp.arange(local_width)
    panel_tiles = PW // tile_size
    stop_col = PW
    pieces = [
        broadcast(matrix[0], ("fem", "row"), 0 * panel_tiles + member)
        for member in range(panel_tiles)
    ]
    panel_top = jnp.concatenate(pieces, axis=0)
    flattened = matrix.reshape(row_tiles * tile_size, local_width)
    diagonal = jnp.where(col_index == 0, panel_top[:, 0:stop_col], jnp.eye(PW, dtype=jnp.float32))
    packed, lower_inv, upper_inv = factor(diagonal)
    panel_cols = jnp.where(col_index == 0, flattened[:, 0:stop_col], 0.0)
    lower_rows = highest(panel_cols, upper_inv)
    packed, lower_inv, lower_rows = (
        broadcast(packed, "col", 0),
        broadcast(lower_inv, "col", 0),
        broadcast(lower_rows, "col", 0),
    )
    upper_rows = highest(lower_inv, panel_top)
    update = highest(lower_rows, upper_rows)
    below_mask = global_rows >= stop_col
    right_mask = global_cols >= stop_col
    rows_inside = (global_rows >= 0) & (global_rows < stop_col)
    cols_inside = (global_cols >= 0) & (global_cols < stop_col)
    lower_full = jnp.zeros(flattened.shape, jnp.float32).at[:, 0:stop_col].set(lower_rows)
    upper_full = jnp.where(col_index == 0, upper_rows.at[:, 0:stop_col].set(packed), upper_rows)
    gathered = upper_full[jnp.clip(global_rows - 0, 0, PW - 1)]
    result = jnp.where(below_mask[:, None] & right_mask[None, :], flattened - update, flattened)
    result = jnp.where(below_mask[:, None] & cols_inside[None, :], lower_full, result)
    result = jnp.where(rows_inside[:, None] & (global_cols >= 0)[None, :], gathered, result)
    matrix = result.reshape(row_tiles, tile_size, local_width)
    return matrix[:, None]


def pair_table(slots):
    pairs = [(a, a) for a in range(slots)]
    pairs += [(a, b) for a in range(slots) for b in range(a + 1, slots)]
    return {pair: place for place, pair in enumerate(pairs)}


def position():
    fem, row, col = lax.axis_index("fem"), lax.axis_index("row"), lax.axis_index("col")
    return fem, row, col, (fem * lax.axis_size("row") + row) * lax.axis_size("col") + col


def schur_kernel(slots, tile, block, tiles_hbm, left_hbm, right_hbm, bem_hbm, first_ref, second_ref, corner_ref,
                 token_ref, left, right, product, flipped, tiles, bem, left_sems, right_sems, small_sems):
    order = left.shape[0]
    steps = order // block
    table = pair_table(slots)
    half = first_ref.shape[0]
    wide = block // tile

    def left_copy(i):
        window = (pl.ds(i * block, block), pl.ds(0, (i + 1) * block))
        return pltpu.make_async_copy(left_hbm.at[(0, *window)], left.at[window], left_sems.at[i])

    def right_copy(i):
        window = pl.ds(i * block, block)
        return pltpu.make_async_copy(right_hbm.at[0, window], right.at[window], right_sems.at[i])

    for i in range(steps):
        right_copy(i).start()
        left_copy(i).start()
    tiles_copy = pltpu.make_async_copy(tiles_hbm, tiles, small_sems.at[0])
    bem_copy = pltpu.make_async_copy(bem_hbm.at[0, 0, :, pl.ds(0, PW)], bem, small_sems.at[1])
    tiles_copy.start()
    bem_copy.start()
    for i in range(steps):
        right_copy(i).wait()
        left_copy(i).wait()
        reach = (i + 1) * block
        rows = jnp.dot(left[i * block:reach, :reach], right[:reach, :],
                       preferred_element_type=jnp.float32).astype(jnp.bfloat16)
        product[i * block:reach, :] = rows
        flipped[:, i * block:reach] = rows.T
    for j in range(slots // wide):
        tall = (j + 1) * block
        part = jnp.dot(flipped[:tall, :], product[:, j * block:tall],
                       preferred_element_type=jnp.float32).astype(jnp.bfloat16)
        for b in range(j * wide, (j + 1) * wide):
            for a in range(b + 1):
                value = part[a * tile:(a + 1) * tile, (b - j * wide) * tile:(b - j * wide + 1) * tile]
                place = table[a, b]
                if place < half:
                    first_ref[place] = value
                else:
                    second_ref[place - half] = value
    fem, row, col, subdomain = position()
    tiles_copy.wait()
    bem_copy.wait()
    corner_ref[...] = jnp.where((fem == 0) & (col == 0), bem[...], 0.0)
    listed = tiles[pl.ds(subdomain, 1), :]
    diag = jnp.zeros((tile, tile), jnp.float32)
    for a in range(slots):
        hit = jnp.broadcast_to(listed[:, a:a + 1], (tile, tile)) == 0
        diag = jnp.where(hit, first_ref[a].astype(jnp.float32), diag)

    for member in range(PW // tile):
        @pl.when(row == member)
        def _():
            corner_ref[:, member * tile:(member + 1) * tile] += diag

    token_ref[0] = 0


def schur(tiles, inverse_factor, coupling, bem_block, slots, tile):
    _, order, width = coupling.shape
    count = len(pair_table(slots))
    half = int(count * SHARE)
    block = 2 * tile
    steps = order // block
    return pl.pallas_call(
        functools.partial(schur_kernel, slots, tile, block),
        out_shape=(jax.ShapeDtypeStruct((half, tile, tile), jnp.bfloat16),
                   jax.ShapeDtypeStruct((count - half, tile, tile), jnp.bfloat16),
                   jax.ShapeDtypeStruct((tile, PW), jnp.float32), jax.ShapeDtypeStruct((1,), jnp.int32)),
        in_specs=[pl.BlockSpec(memory_space=pltpu.HBM)] * 4,
        out_specs=(pl.BlockSpec(),) * 3 + (pl.BlockSpec(memory_space=pltpu.SMEM),),
        scratch_shapes=[pltpu.VMEM((order, order), jnp.bfloat16), pltpu.VMEM((order, width), jnp.bfloat16),
                        pltpu.VMEM((order, width), jnp.bfloat16), pltpu.VMEM((width, order), jnp.bfloat16),
                        pltpu.VMEM(tiles.shape, jnp.int32), pltpu.VMEM((tile, PW), jnp.float32),
                        pltpu.SemaphoreType.DMA((steps,)), pltpu.SemaphoreType.DMA((steps,)),
                        pltpu.SemaphoreType.DMA((2,))],
        compiler_params=pltpu.CompilerParams(vmem_limit_bytes=56 << 20),
        name="schur",
    )(tiles, inverse_factor, coupling, bem_block)


def pick_table(tiles, rows, columns, slots):
    sources = tiles.shape[0]
    count = slots * (slots + 1) // 2

    def slot_of(wanted):
        hit = tiles[None, :, :] == wanted[:, None, None]
        return jnp.max(jnp.where(hit, jnp.arange(slots, dtype=jnp.int32), -1), axis=2)

    a = slot_of(rows)[:, None, :]
    b = slot_of(columns)[None, :, :]
    low, high = jnp.minimum(a, b), jnp.maximum(a, b)
    place = jnp.where(a == b, a, slots + low * (2 * slots - 1 - low) // 2 + high - low - 1)
    place = place + count * jnp.arange(sources, dtype=jnp.int32)
    there = low >= 0
    empty = count * sources
    direct = jnp.where(there & (a <= b), place, empty)
    turned = jnp.where(there & (a > b), place, empty)
    return jnp.stack([direct, turned], axis=2).astype(jnp.int32)


def collect_kernel(sources, lists, table_refs, packs, outs, store, sems):
    count = (store.shape[0] - 1) // sources
    copies = []
    for source in range(sources):
        base = source * count
        for half in range(2):
            ref = packs[2 * source + half]
            size = ref.shape[0]
            copies.append(pltpu.make_async_copy(ref, store.at[pl.ds(base, size)], sems.at[2 * source + half]))
            base += size
    for copy in copies:
        copy.start()
    store[count * sources] = jnp.zeros(store.shape[1:], store.dtype)
    for copy in copies:
        copy.wait()
    for (rows, columns), table, group in zip(lists, table_refs, outs):
        def one(i, carry, columns=columns, table=table, group=group):
            k, m = lax.div(i, columns), lax.rem(i, columns)
            base = i * 2 * sources
            direct = store[table[base]].astype(jnp.float32)
            turned = store[table[base + sources]].astype(jnp.float32)
            for source in range(1, sources):
                direct = direct + store[table[base + source]].astype(jnp.float32)
                turned = turned + store[table[base + sources + source]].astype(jnp.float32)
            total = direct + turned.T
            for ref in group:
                ref[k, m] = total.astype(ref.dtype)
            return carry

        lax.fori_loop(0, rows * columns, one, 0, unroll=2)


def collect(tables, packs, types):
    sources = len(packs)
    flat = [half for pack in packs for half in pack]
    tile = flat[0].shape[-1]
    count = packs[0][0].shape[0] + packs[0][1].shape[0]
    lists = [table.shape[:2] for table in tables]
    shapes = [jax.ShapeDtypeStruct((*dims, tile, tile), kind) for dims, kinds in zip(lists, types) for kind in kinds]

    def kernel(*refs):
        table_refs, refs = refs[:len(tables)], refs[len(tables):]
        pack_refs, refs = refs[:len(flat)], refs[len(flat):]
        groups = []
        for kinds in types:
            groups.append(refs[:len(kinds)])
            refs = refs[len(kinds):]
        store, sems = refs
        collect_kernel(sources, lists, table_refs, pack_refs, groups, store, sems)

    return pl.pallas_call(
        kernel,
        out_shape=tuple(shapes),
        in_specs=[pl.BlockSpec(memory_space=pltpu.SMEM)] * len(tables)
        + [pl.BlockSpec(memory_space=pl.ANY)] * len(flat),
        out_specs=tuple(pl.BlockSpec(memory_space=pltpu.VMEM) for _ in shapes),
        scratch_shapes=[pltpu.VMEM((count * sources + 1, tile, tile), jnp.bfloat16),
                        pltpu.SemaphoreType.DMA((len(flat),))],
        compiler_params=pltpu.CompilerParams(vmem_limit_bytes=52 << 20),
    )(*[table.reshape(-1) for table in tables], *flat)


def split(value):
    high = value.astype(jnp.bfloat16)
    return high, (value - high.astype(jnp.float32)).astype(jnp.bfloat16)


def three_pass(left, right):
    (left_high, left_low), (right_high, right_low) = left, right

    def product(a, b):
        return jnp.dot(a, b, preferred_element_type=jnp.float32)

    return product(left_high, right_high) + (product(left_high, right_low) + product(left_low, right_high))


def panel_kernel(per_block, row_count, lower_hbm, upper_hbm, mine_hbm, other_hbm, mine_strip_hbm, other_strip_hbm,
                 strip_hbm, *refs):
    lefts, refs = refs[:-10], refs[-10:]
    upper_rows_ref, lower_rows_ref, lower_ref, upper_ref, top, extra, strip_ref, cols, sems, left_sems = refs
    _, row, col, _ = position()
    tile = mine_hbm.shape[0]
    count = strip_hbm.shape[0]
    n = lower_ref.shape[0]
    odd = lax.rem(row, 2)
    bases = [pl.multiple_of(residue * tile, tile) for residue in (odd, 1 - odd)]
    pairs = [(lower_hbm, lower_ref), (mine_hbm, top.at[pl.ds(bases[0], tile)]), (mine_strip_hbm, extra.at[0]),
             (other_hbm, top.at[pl.ds(bases[1], tile)]), (other_strip_hbm, extra.at[1]),
             (upper_hbm, upper_ref), (strip_hbm, strip_ref)]
    copies = [pltpu.make_async_copy(source, target, sems.at[i]) for i, (source, target) in enumerate(pairs)]
    for copy in copies:
        copy.start()

    def take(k, source):
        return pltpu.make_async_copy(source.at[k], cols.at[pl.ds(k * tile, tile)], left_sems.at[k])

    for place, source in enumerate(lefts):
        @pl.when(col == place)
        def _():
            for k in range(count):
                take(k, source).start()
    for copy in copies[:5]:
        copy.wait()
    for member, residue in enumerate((odd, 1 - odd)):
        for m in range(per_block):
            lanes = pl.ds(pl.multiple_of((m * row_count + residue) * tile, tile), tile)
            top[pl.ds(bases[member], tile), lanes] += extra[member, m]
    lower = split(lower_ref[...])
    step = 2 * n
    for i in range(top.shape[1] // step):
        upper_rows_ref[:, i * step:(i + 1) * step] = three_pass(lower, split(top[:, i * step:(i + 1) * step]))
    for k in range(count):
        take(k, lefts[0]).wait()
    for copy in copies[5:]:
        copy.wait()

    @pl.when(row < 2)
    def _():
        lanes = pl.ds(pl.multiple_of(odd * tile, tile), tile)
        for k in range(count):
            cols[k * tile:(k + 1) * tile, lanes] += strip_ref[k]

    upper = split(upper_ref[...])
    for i in range(cols.shape[0] // step):
        high, low = split(three_pass(split(cols[i * step:(i + 1) * step, :]), upper))
        lower_rows_ref[i * step:(i + 1) * step, :n] = high
        lower_rows_ref[i * step:(i + 1) * step, n:] = low


def panel(lower, upper, mine, other, mine_strip, other_strip, strip, lefts, per_block, row_count):
    n = lower.shape[0]
    count, tile, _ = lefts[0].shape
    width = mine.shape[1]
    square = pltpu.VMEM((n, n), jnp.float32)
    return pl.pallas_call(
        functools.partial(panel_kernel, per_block, row_count),
        out_shape=(jax.ShapeDtypeStruct((n, width), jnp.float32),
                   jax.ShapeDtypeStruct((count * tile, 2 * n), jnp.bfloat16)),
        in_specs=[pl.BlockSpec(memory_space=pl.ANY)] * (7 + len(lefts)),
        out_specs=(pl.BlockSpec(), pl.BlockSpec()),
        scratch_shapes=[square, square, pltpu.VMEM((n, width), jnp.float32),
                        pltpu.VMEM((2, *mine_strip.shape), jnp.float32), pltpu.VMEM(strip.shape, jnp.float32),
                        pltpu.VMEM((count * tile, n), jnp.float32),
                        pltpu.SemaphoreType.DMA((7,)), pltpu.SemaphoreType.DMA((count,))],
        compiler_params=pltpu.CompilerParams(vmem_limit_bytes=52 << 20),
        name="panel",
    )(lower, upper, mine, other, mine_strip, other_strip, strip, *lefts)


def finish_kernel(row_count, bem_ref, own_ref, lower_ref, upper_ref, packed_ref, out_ref, kept_ref):
    step = pl.program_id(0)
    fem, row, col, _ = position()
    device = fem * row_count + row
    count, _, tile, n = bem_ref.shape
    corner = (col == 0) & (step == 0)

    @pl.when(jnp.logical_not(corner))
    def _():
        high, low = split(upper_ref[...])
        both = jnp.dot(lower_ref[...], jnp.concatenate([high, high], axis=0), preferred_element_type=jnp.float32)
        update = both + jnp.dot(lower_ref[:, :n], low, preferred_element_type=jnp.float32)
        for k in range(count):
            out_ref[k, 0] = bem_ref[k, 0] - update[k * tile:(k + 1) * tile, :]

        @pl.when(device < 2)
        def _():
            out_ref[0, 0] = upper_ref[pl.ds(pl.multiple_of(device * tile, tile), tile), :]

    @pl.when(corner)
    def _():
        for k in range(count):
            rows = slice(k * tile, (k + 1) * tile)
            out_ref[k, 0] = lower_ref[rows, :n].astype(jnp.float32) + lower_ref[rows, n:].astype(jnp.float32)

        @pl.when(device < 2)
        def _():
            out_ref[0, 0] = packed_ref[pl.ds(pl.multiple_of(device * tile, tile), tile), :]

    @pl.when(lax.div(row, 2) == lax.rem(step, 2))
    def _():
        lanes = pl.ds(pl.multiple_of(lax.rem(row, 2) * tile, tile), tile)
        for k in range(count):
            done = corner | (device < 2) if k == 0 else corner
            kept_ref[k, lax.div(step, 2)] = out_ref[k, 0, :, lanes] + jnp.where(done, 0.0, own_ref[k, 0])


def finish(bem_block, own, lower_rows, upper_rows, packed, row_count):
    count, _, tile, width = bem_block.shape
    n = packed.shape[0]
    tiles_wide = n // tile
    whole = lambda shape: pl.BlockSpec(shape, lambda i: (0,) * len(shape))
    contribution = pl.BlockSpec((count, 1, tile, tile), lambda i: (0, i * tiles_wide // row_count, 0, 0))
    wide = pl.BlockSpec((count, 1, tile, n), lambda i: (0, 0, 0, i))
    return pl.pallas_call(
        functools.partial(finish_kernel, row_count),
        grid=(width // n,),
        out_shape=(jax.ShapeDtypeStruct(bem_block.shape, jnp.float32), jax.ShapeDtypeStruct(own.shape, jnp.float32)),
        in_specs=[wide, contribution, whole(lower_rows.shape), pl.BlockSpec((n, n), lambda i: (0, i)),
                  whole(packed.shape)],
        out_specs=(wide, pl.BlockSpec(memory_space=pltpu.VMEM)),
        compiler_params=pltpu.CompilerParams(vmem_limit_bytes=40 << 20),
        name="finish",
    )(bem_block, own, lower_rows, upper_rows, packed)


def patch_kernel(row_count, kept_ref, recv_ref, value_hbm, out_hbm, total, sems):
    fem, row, col, _ = position()
    device = fem * row_count + row
    count, per_block, tile, _ = kept_ref.shape
    copies = []
    for m in range(per_block):
        column = (col == 0) & (row < 2) if m == 0 else jnp.bool_(False)
        for k in range(count):
            done = column | (device < 2) if k == 0 else column
            total[m, k] = kept_ref[k, m] + jnp.where(done, 0.0, recv_ref[k, m].astype(jnp.float32))
        lanes = pl.ds(pl.multiple_of((m * row_count + row) * tile, tile), tile)
        copies.append(pltpu.make_async_copy(total.at[m], out_hbm.at[:, 0, :, lanes], sems.at[m]))
        copies[-1].start()
    for copy in copies:
        copy.wait()


def patch(kept, recv, value, row_count):
    count, per_block, tile, _ = recv.shape
    vmem = pl.BlockSpec(memory_space=pltpu.VMEM)
    return pl.pallas_call(
        functools.partial(patch_kernel, row_count),
        in_specs=[vmem, vmem, pl.BlockSpec(memory_space=pltpu.HBM)],
        out_specs=pl.BlockSpec(memory_space=pltpu.HBM),
        out_shape=jax.ShapeDtypeStruct(value.shape, value.dtype),
        input_output_aliases={2: 0},
        scratch_shapes=[pltpu.VMEM((per_block, count, tile, tile), jnp.float32), pltpu.SemaphoreType.DMA((per_block,))],
        compiler_params=pltpu.CompilerParams(vmem_limit_bytes=24 << 20),
        name="patch",
    )(kept, recv, value)


def local_square(inverse_factor, coupling, boundary_tiles, bem_block):
    return square_plan(inverse_factor, coupling, boundary_tiles, bem_block)


def square_plan(inverse_factor, coupling, boundary_tiles, bem_block):
    fem_count = lax.axis_size("fem")
    row_count = lax.axis_size("row")
    col_count = lax.axis_size("col")
    fem, row, col, _ = position()
    count, _, tile, width = bem_block.shape
    slots = boundary_tiles.shape[1]
    class_tiles = count * fem_count
    per_block = class_tiles // col_count
    swap_fem = [(0, 1), (1, 0)]
    swap_near = [(0, 1), (1, 0), (2, 3), (3, 2)]
    swap_far = [(0, 2), (1, 3), (2, 0), (3, 1)]
    swap_both = [(f * col_count + a, (1 - f) * col_count + b) for f in range(2) for a, b in swap_near]
    near = lambda v: lax.ppermute(v, "col", swap_near)
    far = lambda v: lax.ppermute(v, "col", swap_far)
    across = lambda v: lax.ppermute(v, "fem", swap_fem)
    both = lambda v: lax.ppermute(v, ("fem", "col"), swap_both)
    core = lambda v: lax.ppermute(v, "row", swap_near)
    over = lambda v: lax.ppermute(v, "row", [(0, 2), (1, 3)])
    down = lambda v: lax.ppermute(v, "fem", [(0, 1)])
    hop = lambda place: lambda v: lax.ppermute(v, "col", [(place, place + 1)])

    lefts = [bem_block[:, 0, :, :PW]]
    lefts.append(hop(0)(lefts[0]))

    first, second, corner, token = schur(boundary_tiles, inverse_factor, coupling, bem_block, slots,
                                         tile)

    corner_f, corner_n = across(corner), near(corner)
    corner = (corner + corner_f) + (corner_n + both(corner))

    second_n, first_f = near(second), across(first)
    first_n, second_f = near(first), across(second)
    first_fn = near(first_f)
    second_fn = across(second_n)
    packs = [(first, second), (first_f, second_f), (first_n, second_n), (first_fn, second_fn)]

    rows = lax.dynamic_slice(bem_block, (token[0], 0, 0, 0), (1, 1, tile, width))[0, 0]
    rows_over = over(rows)
    lefts.append(hop(1)(lefts[1]))

    corner = jnp.where(row >= 2, over(corner), corner)
    corner_other = core(corner)
    odd = row % 2 == 1
    square = jnp.concatenate([jnp.where(odd, corner_other, corner), jnp.where(odd, corner, corner_other)], axis=0)
    square = square + far(square)
    packed, lower_inv, upper_inv = factor(square)

    def tiles_of(f, c):
        return lax.dynamic_index_in_dim(boundary_tiles, (f * row_count + row) * col_count + c, 0, keepdims=False)

    near_col = col + 1 - 2 * (col % 2)
    far_col = (col + 2) % 4
    tiles = jnp.stack([tiles_of(fem, col), tiles_of(1 - fem, col), tiles_of(fem, near_col), tiles_of(1 - fem, near_col)])
    tiles = tiles + token[0]
    held = jnp.arange(count, dtype=jnp.int32) * fem_count + fem
    block_cols = jnp.arange(per_block, dtype=jnp.int32)
    share = per_block // fem_count
    columns = jnp.concatenate([far_col * per_block + block_cols, col * per_block + block_cols,
                               jnp.zeros((1,), jnp.int32)])
    table = pick_table(tiles, held, columns, slots)
    far_table, own_table, strip_table = table[:, :per_block], table[:, per_block:2 * per_block], table[:, 2 * per_block:]

    cross, strip, strip_send = collect([far_table, strip_table], packs,
                                     [(jnp.bfloat16,), (jnp.float32, jnp.bfloat16)])
    strip = strip[:, 0]
    strip_far = far(strip_send[:, 0])
    lefts.append(hop(2)(after(lefts[2], cross)))
    rows_all = jnp.where(row >= 2, after(rows_over, cross), rows)
    rows_down = down(rows_all)
    own_table = after(own_table, cross)
    own, = collect([own_table], packs, [(jnp.float32,)])

    strip = strip + after(strip_far, own).astype(jnp.float32)
    recv = far(after(cross, strip))
    local_strip = jnp.swapaxes(lax.dynamic_slice_in_dim(strip, col * share, share, 0), 1, 2)
    turned = across(local_strip)
    even = jnp.where(fem == 0, local_strip, turned)
    other = jnp.where(fem == 0, turned, local_strip)
    top_strip = jnp.stack([even, other], axis=1).reshape(per_block, tile, tile)
    top_strip = jnp.where(row >= 2, over(top_strip), top_strip)
    top_other = core(top_strip)
    rows_all = jnp.where(fem == 1, after(rows_down, top_strip), rows_all)
    rows_other = core(rows_all)
    upper_rows, lower_rows = panel(lower_inv, upper_inv, rows_all, rows_other, top_strip, top_other,
                                   strip, lefts, per_block, row_count)
    value, kept = finish(bem_block, own, lower_rows, upper_rows, packed, row_count)
    return patch(kept, recv, value, row_count)


def solution(mesh):
    placed = (
        P(("fem", "row", "col"), None, None),
        P(("fem", "row", "col"), None, None),
        P(),
        P(None, ("fem", "row"), None, "col"),
    )
    sizes = dict(mesh.shape)
    square = sizes["fem"] == 2 and sizes["row"] == 4 and sizes["col"] == 4
    return jax.shard_map(
        local_square if square else local,
        mesh=mesh,
        in_specs=placed,
        out_specs=P(None, ("fem", "row"), None, "col"),
        check_vma=False,
    )
```
